256 devices in a mesh: freq: 64 (over x, y_hi, z), space: 4 (over y_lo, core).
Axes of the slice: x: 4, y: 4 (y_hi: 2, y_lo: 2; y = y_hi * 2 + y_lo), z: 8, core: 2. Of those that a mesh axis runs over, the one named last changes fastest.
Arguments:
- modes: bfloat16 [8, 64, 2, 3, 24, 512], P(None, 'freq', None, None, None, 'space'), may hold values from -3 to 3
- point_weights: float32 [512], P('space'), may hold values from 0.25 to 4
- triads: int32 [8, 64, 16], P(None, 'freq'), may hold values from 0 to 511, as said below
- counts: int32 [8, 64], P(None, 'freq'), may hold values from 1 to 16, as said below
Outputs:
- grams: float32 [8, 64, 16, 1152], P(None, 'freq')
The draws below stay inside these ranges and needn't reach their ends.
Inputs may be any that keep to these rules, and one draw needn't show every extreme that they name: `triads`: for each column c, its 128 entries (those beyond a bin's count included) hold, for every residue e modulo 64, exactly 2 values l with l mod 64 = e. `counts`: in every draw all reader bins of some column c have 16 live triads.
All inputs are finite; a program needn't handle non-finite values.
Results may differ from the reference program's by a relative error of at most 0.0029.
Values may be sent and summed in bfloat16 or wider, within the bound.
No kernel may reach another device: no remote copies, remote signals or barrier semaphores. Data moves between devices by JAX's collectives and lax.ppermute only.
A program may use at most 64 MiB of HBM per device.

```python
import math
import jax
import jax.numpy as jnp
from jax import lax

NB = 24
NC = 3
BD = 8
TMAX = 16
STRIDE = 64
NPTS = 512


def draw_triads(key, part):
    entries = BD * TMAX

    def one_device(device_index):
        device_key = jax.random.fold_in(key, device_index)
        shuffled = jax.random.permutation(jax.random.fold_in(device_key, 1), entries)
        owners = shuffled % STRIDE
        rows_drawn = jax.random.randint(jax.random.fold_in(device_key, 2), (entries,), 0, BD)
        return (rows_drawn * STRIDE + owners).reshape(BD, TMAX).astype(jnp.int32)
    stacked = jax.vmap(one_device)(jnp.arange(STRIDE))
    return jnp.transpose(stacked, (1, 0, 2))


def draw_counts(key, part):
    drawn = jax.random.randint(jax.random.fold_in(key, 3), (BD, STRIDE), 1, TMAX + 1)
    chosen = jax.random.randint(jax.random.fold_in(key, 4), (), 0, STRIDE)
    column = jnp.arange(STRIDE)[None, :]
    return jnp.where(column == chosen, TMAX, drawn).astype(jnp.int32)


def steps_of(rng, dims, cuts, least, high):
    level = 1.0
    for position, parts in cuts:
        draws = jax.random.uniform(jax.random.fold_in(jax.random.fold_in(rng, 6), position), (parts,), jnp.float32, least / len(cuts), high / len(cuts))
        level = level * jnp.repeat(jnp.exp(draws), dims[position] // parts).reshape((-1,) + (1,) * (len(dims) - 1 - position))
    return level


def centred(own_key, dims, scale, bound, cuts=(), kind=jnp.bfloat16):
    factor_of = steps_of(own_key, dims, cuts, -0.22, 0.18) if cuts else 1.0
    values = jax.random.normal(own_key, dims, jnp.float32) * scale * factor_of
    return jnp.minimum(jnp.maximum(values, -bound), bound).astype(kind)


def setup_inputs(seed: int = 0) -> dict:
    key_of = jax.random.split(jax.random.key(seed), 5)
    return {
        "modes": centred(key_of[0], (BD, STRIDE, 2, NC, NB, NPTS), 0.5, 3.0, ((1, 64), (5, 4))),
        "point_weights": jnp.clip(jnp.exp(math.log(4.0) - 2.7725887 * jax.random.uniform(key_of[1], (NPTS,), jnp.float32) ** steps_of(key_of[1], (NPTS,), ((0, 4),), -0.2, 0.2)), 0.25, 4.0),
        "triads": draw_triads(jax.random.fold_in(key_of[4], 71), 0),
        "counts": draw_counts(jax.random.fold_in(key_of[4], 71), 0),
    }


def reference(modes, point_weights, triads, counts):
    all_bins = BD * STRIDE
    flat_modes = modes.reshape(all_bins, 2, NC, NB, NPTS)
    entry_lists = triads.reshape(all_bins, TMAX)
    live_counts = counts.reshape(all_bins)
    positions = jnp.arange(TMAX, dtype=jnp.int32)

    def one_bin(bin_index):
        first_block = flat_modes[bin_index].astype(jnp.float32)
        listed = entry_lists[bin_index]
        seconds = flat_modes[listed].astype(jnp.float32)
        sum_bins = ((bin_index + listed) % all_bins).astype(jnp.int32)
        thirds = flat_modes[sum_bins].astype(jnp.float32)
        real_part = first_block[0] * seconds[:, 0] - first_block[1] * seconds[:, 1]
        imag_part = -(first_block[0] * seconds[:, 1] + first_block[1] * seconds[:, 0])
        weighted = jnp.stack([real_part, imag_part], axis=1) * point_weights
        weighted = weighted.astype(jnp.bfloat16).astype(jnp.float32)
        products = jnp.einsum('tacjp,tbckp->tabjk', weighted, thirds, precision=lax.Precision.HIGHEST)
        gram_real = products[:, 0, 0] - products[:, 1, 1]
        gram_imag = products[:, 0, 1] + products[:, 1, 0]
        result = jnp.stack([gram_real, gram_imag], axis=1).reshape(TMAX, 2 * NB * NB) / NB
        live_mask = (positions < live_counts[bin_index]).astype(jnp.float32)
        return result * live_mask[:, None]

    mapped = lax.map(one_bin, jnp.arange(all_bins, dtype=jnp.int32))
    return mapped.reshape(BD, STRIDE, TMAX, 2 * NB * NB)
```

```python
import functools

import jax
import jax.numpy as jnp
from jax import lax
from jax.experimental import pallas as pl
from jax.experimental.pallas import tpu as pltpu
from jax.sharding import Mesh
from jax.sharding import PartitionSpec as P

F32, BF16 = jnp.float32, jnp.bfloat16
LANES = 128
VMEM_LIMIT = 56 * 1024 * 1024


def split_kernel(place_ref, x_ref, out_ref):
    place = place_ref[0]
    block = lax.broadcasted_iota(jnp.int32, (24, LANES), 1) // 16
    for q in range(6):
        sources = [x_ref[8 * q + s].astype(F32) for s in range(8)]
        for piece in range(8):
            built = None
            for s in range(8):
                shift = (s - piece) % 8 * 16
                moved = pltpu.roll(sources[s], shift, 1) if shift else sources[s]
                built = moved if built is None else jnp.where(block == s, moved, built)
            out_ref[(piece - place) & 7, q] = built.astype(BF16)


def unpack_column(own, sib, bins_ref, first_bin):
    lane = lax.broadcasted_iota(jnp.int32, (24, LANES), 1)
    tiles = [[ref[q].astype(F32) for q in range(6)] for ref in (own, sib)]
    for r in range(8):
        for part in range(2):
            q, offset = divmod(96 * r + 48 * part, LANES)
            halves = []
            for core in range(2):
                picked = tiles[core][q]
                if offset + 48 > LANES:
                    picked = jnp.where(lane >= offset, picked, tiles[core][q + 1])
                shift = (48 * core - offset) % LANES
                halves.append(pltpu.roll(picked, shift, 1) if shift else picked)
            merged = jnp.where(lane < 48, halves[0], halves[1])
            bins_ref[first_bin + r, :, LANES * part : LANES * (part + 1)] = merged.astype(BF16)


def grams_kernel(meta_ref, triads_ref, weights_ref, *refs):
    own_refs, sib_refs = refs[:9], refs[9:18]
    out_ref, bins_ref, w_ref, q_ref = refs[18:]
    place, depth, core = meta_ref[0], meta_ref[1], meta_ref[2]

    for index, turn in enumerate((0, 1, 2, 3, 5, 6, 7)):

        @pl.loop(0, 8)
        def _(d, index=index, turn=turn):
            unpack_column(
                own_refs[index].at[d], sib_refs[index].at[d], bins_ref, turn * 64 + d * 8
            )

    for half in range(2):

        @pl.loop(0, 4)
        def _(d, half=half):
            unpack_column(
                own_refs[7 + half].at[d],
                sib_refs[7 + half].at[d],
                bins_ref,
                4 * 64 + half * 32 + d * 8,
            )

    def slot(which):
        return (
            ((depth - (which & 7)) & 7) * 64
            + ((place - ((which >> 3) & 7)) & 7) * 8
            + (which >> 6)
        )

    weights = weights_ref[0:1, :]
    lane = lax.broadcasted_iota(jnp.int32, (48, LANES), 1)

    @pl.loop(0, 32)
    def _(reader):
        d = reader >> 2
        owner_half = (reader >> 1) & 1
        sub = reader & 1
        row = owner_half * 4 + core * 2 + sub
        owner = (place - d) & 7
        k_bin = row * 64 + owner * 8 + depth
        first = bins_ref[d * 8 + row].astype(F32)
        k_real = first[:, :LANES] * weights
        k_imag = first[:, LANES:] * weights
        for t in range(16):
            l_bin = triads_ref[d, row * 16 + t]
            m_bin = (k_bin + l_bin) & 511
            second = bins_ref[slot(l_bin)].astype(F32)
            l_real, l_imag = second[:, :LANES], second[:, LANES:]
            real = (k_real * l_real - k_imag * l_imag).astype(BF16)
            imag = k_real * l_imag + k_imag * l_real
            plus, minus = imag.astype(BF16), (-imag).astype(BF16)
            w_ref[48 * t : 48 * t + 24, :LANES] = real
            w_ref[48 * t : 48 * t + 24, LANES:] = plus
            w_ref[48 * t + 24 : 48 * t + 48, :LANES] = minus
            w_ref[48 * t + 24 : 48 * t + 48, LANES:] = real
            q_ref[24 * t : 24 * t + 24, :] = bins_ref[slot(m_bin)]
        for n in range(3):
            start = 5 * n
            product = lax.dot_general(
                w_ref[48 * start : 48 * (start + 6), :],
                q_ref[LANES * n : LANES * (n + 1), :],
                (((1,), (1,)), ((), ())),
                preferred_element_type=F32,
            )
            built = product[:48]
            for i in range(1, 6):
                begin = 24 * (start + i) - LANES * n
                built = jnp.where(lane >= begin, product[48 * i : 48 * (i + 1)], built)
            out_ref[owner * 2 + owner_half, sub, :, LANES * n : LANES * (n + 1)] = built.astype(
                BF16
            )


def vmem():
    return pl.BlockSpec(memory_space=pltpu.VMEM)


def smem():
    return pl.BlockSpec(memory_space=pltpu.SMEM)


def step(array, axes, by):
    size = lax.axis_size(axes)
    return lax.ppermute(array, axes, [(i, (i + by) % size) for i in range(size)])


def body(modes, point_weights, triads, counts):
    plane = ("x", "yh")
    place, depth, core = lax.axis_index(plane), lax.axis_index("z"), lax.axis_index("core")
    half = lax.axis_index("yl")

    pieces = pl.pallas_call(
        split_kernel,
        out_shape=jax.ShapeDtypeStruct((8, 6, 24, LANES), BF16),
        in_specs=[smem(), vmem()],
        out_specs=vmem(),
        compiler_params=pltpu.CompilerParams(vmem_limit_bytes=VMEM_LIMIT),
        name="split",
    )(place.astype(jnp.int32)[None], modes.reshape(48, 24, LANES))

    block = jnp.stack([pieces[0]] + [step(pieces[d], plane, d) for d in range(1, 8)])
    lists = triads.reshape(128)
    all_lists = jnp.stack([lists] + [step(lists, plane, d) for d in range(1, 8)])

    own_weights = lax.dynamic_slice_in_dim(point_weights, place * 16, 16)
    sib_weights = step(own_weights, "core", 1)
    lane_weights = jnp.concatenate([own_weights] * 3 + [sib_weights] * 3 + [jnp.zeros(32, F32)])

    ahead, behind = [block], [block]
    for _ in range(3):
        ahead.append(step(ahead[-1], "z", 1))
        behind.append(step(behind[-1], "z", -1))
    far = [step(ahead[3][:4], "z", 1), step(behind[3][4:], "z", -1)]
    own = ahead + behind[:0:-1] + far
    sib = [step(array, "core", 1) for array in own]

    meta = jnp.stack([place, depth, core]).astype(jnp.int32)
    partial = pl.pallas_call(
        grams_kernel,
        out_shape=jax.ShapeDtypeStruct((16, 2, 48, 384), BF16),
        in_specs=[smem(), smem(), vmem()] + [vmem()] * 18,
        out_specs=vmem(),
        scratch_shapes=[
            pltpu.VMEM((512, 24, 256), BF16),
            pltpu.VMEM((768, 256), BF16),
            pltpu.VMEM((384, 256), BF16),
        ],
        compiler_params=pltpu.CompilerParams(vmem_limit_bytes=VMEM_LIMIT),
        name="grams",
    )(meta, all_lists, jnp.broadcast_to(lane_weights, (8, LANES)), *own, *sib)

    received = lax.all_to_all(partial, ("x", "yh", "yl"), 0, 0)
    summed = jnp.sum(received.astype(F32), axis=0) / 24
    rows = summed.reshape(2, 48, 16, 24).transpose(0, 2, 1, 3).reshape(2, 16, 1152)
    live = lax.dynamic_slice_in_dim(counts[:, 0], 4 * half + 2 * core, 2)
    mask = jnp.arange(16, dtype=jnp.int32)[None, :] < live[:, None]
    rows = rows * mask.astype(F32)[:, :, None]
    return lax.all_gather(rows, ("yl", "core")).reshape(8, 1, 16, 1152)


def solution(mesh):
    fine = Mesh(mesh.devices.reshape(4, 2, 8, 2, 2), ("x", "yh", "z", "yl", "core"))
    freq, space = ("x", "yh", "z"), ("yl", "core")
    return jax.shard_map(
        body,
        mesh=fine,
        in_specs=(
            P(None, freq, None, None, None, space),
            P(space),
            P(None, freq, None),
            P(None, freq),
        ),
        out_specs=P(None, freq, None, None),
        check_vma=False,
    )
```

```python
import functools

import jax
import jax.numpy as jnp
from jax import lax
from jax.experimental import pallas as pl
from jax.experimental.pallas import tpu as pltpu
from jax.sharding import Mesh
from jax.sharding import PartitionSpec as P

F32, BF16 = jnp.float32, jnp.bfloat16
LANES = 128
VMEM_LIMIT = 56 * 1024 * 1024


def split_kernel(x_ref, triads_ref, weights_ref, out_ref):
    block = lax.broadcasted_iota(jnp.int32, (24, LANES), 1) // 16
    for q in range(6):
        sources = [x_ref[8 * q + s].astype(F32) for s in range(8)]
        for piece in range(8):
            built = None
            for s in range(8):
                shift = (s - piece) % 8 * 16
                moved = pltpu.roll(sources[s], shift, 1) if shift else sources[s]
                built = moved if built is None else jnp.where(block == s, moved, built)
            out_ref[piece, 24 * q : 24 * q + 24] = built.astype(BF16)
    listed = triads_ref[...]
    rest = weights_ref[...]
    parts = []
    for _ in range(3):
        parts.append(rest.astype(BF16))
        rest = rest - parts[-1].astype(F32)
    for piece in range(8):
        tile = [(listed >> 6).astype(F32), (listed & 63).astype(F32)]
        for part in parts:
            own = part[:, 16 * piece : 16 * piece + 16].astype(F32)
            tile.append(jnp.broadcast_to(own, (8, 16)))
        tile.append(jnp.zeros((8, 48), F32))
        out_ref[piece, 144:152] = jnp.concatenate(tile, axis=1).astype(BF16)


def unpack_kernel(own_ref, sib_ref, *refs):
    bins_ref = refs[-1]
    lane = lax.broadcasted_iota(jnp.int32, (24, LANES), 1)

    @pl.loop(0, 8)
    def _(column):
        tiles = [
            [ref[column, 24 * q : 24 * q + 24].astype(F32) for q in range(6)]
            for ref in (own_ref, sib_ref)
        ]
        for r in range(8):
            for part in range(2):
                q, offset = divmod(96 * r + 48 * part, LANES)
                halves = []
                for core in range(2):
                    picked = tiles[core][q]
                    if offset + 48 > LANES:
                        picked = jnp.where(lane >= offset, picked, tiles[core][q + 1])
                    shift = (48 * core - offset) % LANES
                    halves.append(pltpu.roll(picked, shift, 1) if shift else picked)
                merged = jnp.where(lane < 48, halves[0], halves[1])
                lanes = slice(LANES * part, LANES * (part + 1))
                bins_ref[column * 8 + r, :, lanes] = merged.astype(BF16)


def lane_weights(own_ref, sib_ref):
    lane = lax.broadcasted_iota(jnp.int32, (8, LANES), 1)
    total = jnp.zeros((8, LANES), F32)
    for core, ref in enumerate((own_ref, sib_ref)):
        tile = ref[...].astype(F32)
        for component in range(3):
            begin = 48 * core + 16 * component
            inside = (lane >= begin) & (lane < begin + 16)
            value = sum(pltpu.roll(tile, (begin - 32 - 16 * n) % LANES, 1) for n in range(3))
            total = jnp.where(inside, value, total)
    return total[0:1]


def grams_kernel(sub, triads_ref, own_w_ref, sib_w_ref, bins_ref, out_ref, w_ref, q_ref):
    place = lax.axis_index("x") * 2 + lax.axis_index("yh")
    depth, core = lax.axis_index("z"), lax.axis_index("core")
    up = 1 - 2 * core

    def slot(which):
        turn = (up * (depth - (which & 7))) & 7
        return turn * 64 + (which & 56) + (which >> 6)

    weights = lane_weights(own_w_ref, sib_w_ref)
    lane = lax.broadcasted_iota(jnp.int32, (48, LANES), 1)

    @pl.loop(0, 16)
    def _(reader):
        owner = reader >> 1
        row = (reader & 1) * 4 + core * 2 + sub
        k_bin = row * 64 + owner * 8 + depth
        first = bins_ref[owner * 8 + row].astype(F32)
        k_real = first[:, :LANES] * weights
        k_imag = first[:, LANES:] * weights
        for t in range(16):
            l_bin = triads_ref[owner * 8 + row, t]
            m_bin = (k_bin + l_bin) & 511
            second = bins_ref[slot(l_bin)].astype(F32)
            l_real, l_imag = second[:, :LANES], second[:, LANES:]
            real = (k_real * l_real - k_imag * l_imag).astype(BF16)
            imag = k_real * l_imag + k_imag * l_real
            plus, minus = imag.astype(BF16), (-imag).astype(BF16)
            w_ref[48 * t : 48 * t + 24, :LANES] = real
            w_ref[48 * t : 48 * t + 24, LANES:] = plus
            w_ref[48 * t + 24 : 48 * t + 48, :LANES] = minus
            w_ref[48 * t + 24 : 48 * t + 48, LANES:] = real
            q_ref[24 * t : 24 * t + 24, :] = bins_ref[slot(m_bin)]
        for n in range(3):
            start = 5 * n
            product = lax.dot_general(
                w_ref[48 * start : 48 * (start + 6), :],
                q_ref[LANES * n : LANES * (n + 1), :],
                (((1,), (1,)), ((), ())),
                preferred_element_type=F32,
            )
            built = product[:48]
            for i in range(1, 6):
                begin = 24 * (start + i) - LANES * n
                built = jnp.where(lane >= begin, product[48 * i : 48 * (i + 1)], built)
            out_ref[reader, :, LANES * n : LANES * (n + 1)] = built.astype(BF16)


def vmem():
    return pl.BlockSpec(memory_space=pltpu.VMEM)


def smem():
    return pl.BlockSpec(memory_space=pltpu.SMEM)


def step(array, axes, by):
    size = lax.axis_size(axes)
    return lax.ppermute(array, axes, [(i, (i + by) % size) for i in range(size)])


def swap(array):
    return step(array, "core", 1)


def ring(array):
    pairs = []
    for z in range(8):
        pairs += [(2 * z, (2 * z + 2) % 16), (2 * z + 1, (2 * z - 2) % 16 + 1)]
    return lax.ppermute(array, ("z", "core"), pairs)


PARAMS = pltpu.CompilerParams(vmem_limit_bytes=VMEM_LIMIT)
BINS = jax.ShapeDtypeStruct((512, 24, 256), BF16)


def unpack(own, sib, bins, turn):
    operands = [own, sib] + ([] if bins is None else [bins])
    return pl.pallas_call(
        unpack_kernel,
        out_shape=BINS,
        grid=(1,),
        in_specs=[pl.BlockSpec((8, 144, LANES), lambda i: (0, 0, 0))] * 2
        + [pl.BlockSpec(memory_space=pl.ANY)] * (len(operands) - 2),
        out_specs=pl.BlockSpec((64, 24, 256), lambda i: (turn, 0, 0)),
        input_output_aliases={} if bins is None else {2: 0},
        compiler_params=PARAMS,
        cost_estimate=pl.CostEstimate(flops=2000000, bytes_accessed=2000000, transcendentals=0),
        name="unpack",
    )(*operands)


def grams(sub, lists, own_tile, sib_tile, bins):
    return pl.pallas_call(
        functools.partial(grams_kernel, sub),
        out_shape=jax.ShapeDtypeStruct((16, 48, 384), BF16),
        in_specs=[smem()] + [vmem()] * 3,
        out_specs=vmem(),
        scratch_shapes=[pltpu.VMEM((768, 256), BF16), pltpu.VMEM((384, 256), BF16)],
        compiler_params=PARAMS,
        cost_estimate=pl.CostEstimate(
            flops=8000000000, bytes_accessed=8000000, transcendentals=0
        ),
        name="grams",
    )(lists, own_tile, sib_tile, bins)


def body(modes, point_weights, triads, counts):
    core, half = lax.axis_index("core"), lax.axis_index("yl")
    pieces = pl.pallas_call(
        split_kernel,
        out_shape=jax.ShapeDtypeStruct((8, 152, LANES), BF16),
        in_specs=[vmem()] * 3,
        out_specs=vmem(),
        compiler_params=PARAMS,
        name="split",
    )(modes.reshape(48, 24, LANES), triads[:, 0], point_weights[None])
    received = lax.all_to_all(pieces, ("x", "yh"), 0, 0)
    tiles = received[:, 144:]
    codes = tiles[:, :, :32].astype(F32)
    lists = (codes[:, :, :16] * 64 + codes[:, :, 16:]).astype(jnp.int32).reshape(64, 16)

    near = [received[:, :144]]
    sib = [swap(near[0])]
    own_tile, sib_tile = tiles[0], swap(tiles[0])
    for _ in range(3):
        near.append(ring(near[-1]))
        sib.append(ring(sib[-1]))
    near.append(ring(near[-1]))
    bins = unpack(near[0], sib[0], None, 0)
    for s in range(1, 4):
        bins = unpack(near[s], sib[s], bins, s)
        bins = unpack(swap(sib[s]), swap(near[s]), bins, 8 - s)
    bins = unpack(near[4], swap(near[4]), bins, 4)

    live = lax.dynamic_slice_in_dim(counts[:, 0], 4 * half + 2 * core, 2)
    mask = (jnp.arange(16, dtype=jnp.int32)[None, :] < live[:, None]).astype(F32)
    rows = []
    for sub in range(2):
        partial = grams(sub, lists, own_tile, sib_tile, bins)
        parts = lax.all_to_all(partial, ("x", "yh", "yl"), 0, 0)
        summed = jnp.sum(parts.astype(F32), axis=0) / 24
        flat = summed.reshape(48, 16, 24).transpose(1, 0, 2).reshape(16, 1152)
        rows.append(flat * mask[sub][:, None])
    return lax.all_gather(jnp.stack(rows), ("yl", "core")).reshape(8, 1, 16, 1152)


def solution(mesh):
    fine = Mesh(mesh.devices.reshape(4, 2, 8, 2, 2), ("x", "yh", "z", "yl", "core"))
    freq, space = ("x", "yh", "z"), ("yl", "core")
    return jax.shard_map(
        body,
        mesh=fine,
        in_specs=(
            P(None, freq, None, None, None, space),
            P(space),
            P(None, freq, None),
            P(None, freq),
        ),
        out_specs=P(None, freq, None, None),
        check_vma=False,
    )
```

```python
import functools

import jax
import jax.numpy as jnp
from jax import lax
from jax.experimental import pallas as pl
from jax.experimental.pallas import tpu as pltpu
from jax.sharding import Mesh
from jax.sharding import PartitionSpec as P

F32, BF16 = jnp.float32, jnp.bfloat16
LANES = 128
MIB = 1024 * 1024


def split_kernel(x_ref, triads_ref, weights_ref, out_ref):
    block = lax.broadcasted_iota(jnp.int32, (24, LANES), 1) // 16
    for q in range(6):
        sources = [x_ref[8 * q + s].astype(F32) for s in range(8)]
        for piece in range(8):
            built = None
            for s in range(8):
                shift = (s - piece) % 8 * 16
                moved = pltpu.roll(sources[s], shift, 1) if shift else sources[s]
                built = moved if built is None else jnp.where(block == s, moved, built)
            out_ref[piece, 24 * q : 24 * q + 24] = built.astype(BF16)
    listed = triads_ref[...]
    rest = weights_ref[...]
    parts = []
    for _ in range(3):
        parts.append(rest.astype(BF16))
        rest = rest - parts[-1].astype(F32)
    for piece in range(8):
        tile = [(listed >> 6).astype(F32), (listed & 63).astype(F32)]
        for part in parts:
            own = part[:, 16 * piece : 16 * piece + 16].astype(F32)
            tile.append(jnp.broadcast_to(own, (8, 16)))
        tile.append(jnp.zeros((8, 48), F32))
        out_ref[piece, 144:152] = jnp.concatenate(tile, axis=1).astype(BF16)


def unpack_kernel(own_ref, sib_ref, *refs):
    bins_ref = refs[-1]
    lane = lax.broadcasted_iota(jnp.int32, (24, LANES), 1)

    @pl.loop(0, 8)
    def _(column):
        tiles = [
            [ref[column, 24 * q : 24 * q + 24].astype(F32) for q in range(6)]
            for ref in (own_ref, sib_ref)
        ]
        for r in range(8):
            for part in range(2):
                q, offset = divmod(96 * r + 48 * part, LANES)
                halves = []
                for core in range(2):
                    picked = tiles[core][q]
                    if offset + 48 > LANES:
                        picked = jnp.where(lane >= offset, picked, tiles[core][q + 1])
                    shift = (48 * core - offset) % LANES
                    halves.append(pltpu.roll(picked, shift, 1) if shift else picked)
                merged = jnp.where(lane < 48, halves[0], halves[1])
                lanes = slice(LANES * part, LANES * (part + 1))
                bins_ref[column * 8 + r, :, lanes] = merged.astype(BF16)


def lane_weights(own_ref, sib_ref):
    lane = lax.broadcasted_iota(jnp.int32, (8, LANES), 1)
    total = jnp.zeros((8, LANES), F32)
    for core, ref in enumerate((own_ref, sib_ref)):
        tile = ref[...].astype(F32)
        for component in range(3):
            begin = 48 * core + 16 * component
            inside = (lane >= begin) & (lane < begin + 16)
            value = sum(pltpu.roll(tile, (begin - 32 - 16 * n) % LANES, 1) for n in range(3))
            total = jnp.where(inside, value, total)
    return total[0:1]


def grams_kernel(sub, triads_ref, own_w_ref, sib_w_ref, bins_ref, out_ref, w_ref, q_ref):
    place = lax.axis_index("x") * 2 + lax.axis_index("yh")
    depth, core = lax.axis_index("z"), lax.axis_index("core")
    up = 1 - 2 * core

    def slot(which):
        turn = (up * (depth - (which & 7))) & 7
        return turn * 64 + (which & 56) + (which >> 6)

    weights = lane_weights(own_w_ref, sib_w_ref)
    lane = lax.broadcasted_iota(jnp.int32, (48, LANES), 1)

    @pl.loop(0, 16)
    def _(reader):
        owner = reader >> 1
        row = (reader & 1) * 4 + core * 2 + sub
        k_bin = row * 64 + owner * 8 + depth
        first = bins_ref[owner * 8 + row].astype(F32)
        k_real = first[:, :LANES] * weights
        k_imag = first[:, LANES:] * weights
        for t in range(16):
            l_bin = triads_ref[owner * 8 + row, t]
            m_bin = (k_bin + l_bin) & 511
            second = bins_ref[slot(l_bin)].astype(F32)
            l_real, l_imag = second[:, :LANES], second[:, LANES:]
            real = (k_real * l_real - k_imag * l_imag).astype(BF16)
            imag = k_real * l_imag + k_imag * l_real
            plus, minus = imag.astype(BF16), (-imag).astype(BF16)
            w_ref[48 * t : 48 * t + 24, :LANES] = real
            w_ref[48 * t : 48 * t + 24, LANES:] = plus
            w_ref[48 * t + 24 : 48 * t + 48, :LANES] = minus
            w_ref[48 * t + 24 : 48 * t + 48, LANES:] = real
            q_ref[24 * t : 24 * t + 24, :] = bins_ref[slot(m_bin)]
        for n in range(3):
            start = 5 * n
            product = lax.dot_general(
                w_ref[48 * start : 48 * (start + 6), :],
                q_ref[LANES * n : LANES * (n + 1), :],
                (((1,), (1,)), ((), ())),
                preferred_element_type=F32,
            )
            built = product[:48]
            for i in range(1, 6):
                begin = 24 * (start + i) - LANES * n
                built = jnp.where(lane >= begin, product[48 * i : 48 * (i + 1)], built)
            out_ref[reader, :, LANES * n : LANES * (n + 1)] = built.astype(BF16)


def vmem():
    return pl.BlockSpec(memory_space=pltpu.VMEM)


def smem():
    return pl.BlockSpec(memory_space=pltpu.SMEM)


def step(array, axes, by):
    size = lax.axis_size(axes)
    return lax.ppermute(array, axes, [(i, (i + by) % size) for i in range(size)])


def swap(array):
    return step(array, "core", 1)


def ring(array):
    pairs = []
    for z in range(8):
        pairs += [(2 * z, (2 * z + 2) % 16), (2 * z + 1, (2 * z - 2) % 16 + 1)]
    return lax.ppermute(array, ("z", "core"), pairs)


def params(mib):
    return pltpu.CompilerParams(vmem_limit_bytes=mib * MIB)


BINS = jax.ShapeDtypeStruct((512, 24, 256), BF16)


def unpack(own, sib, bins, turn):
    operands = [own, sib] + ([] if bins is None else [bins])
    return pl.pallas_call(
        unpack_kernel,
        out_shape=BINS,
        grid=(1,),
        in_specs=[pl.BlockSpec((8, 144, LANES), lambda i: (0, 0, 0))] * 2
        + [pl.BlockSpec(memory_space=pl.ANY)] * (len(operands) - 2),
        out_specs=pl.BlockSpec((64, 24, 256), lambda i: (turn, 0, 0)),
        input_output_aliases={} if bins is None else {2: 0},
        compiler_params=params(8),
        cost_estimate=pl.CostEstimate(flops=4000000000, bytes_accessed=2000000, transcendentals=0),
        name="unpack",
    )(*operands)


def grams(sub, lists, own_tile, sib_tile, bins):
    return pl.pallas_call(
        functools.partial(grams_kernel, sub),
        out_shape=jax.ShapeDtypeStruct((16, 48, 384), BF16),
        in_specs=[smem()] + [vmem()] * 3,
        out_specs=vmem(),
        scratch_shapes=[pltpu.VMEM((768, 256), BF16), pltpu.VMEM((384, 256), BF16)],
        compiler_params=params(16),
        cost_estimate=pl.CostEstimate(
            flops=8000000000, bytes_accessed=8000000, transcendentals=0
        ),
        name="grams",
    )(lists, own_tile, sib_tile, bins)


def body(modes, point_weights, triads, counts):
    core, half = lax.axis_index("core"), lax.axis_index("yl")
    pieces = pl.pallas_call(
        split_kernel,
        out_shape=jax.ShapeDtypeStruct((8, 152, LANES), BF16),
        in_specs=[vmem()] * 3,
        out_specs=vmem(),
        compiler_params=params(8),
        name="split",
    )(modes.reshape(48, 24, LANES), triads[:, 0], point_weights[None])
    received = lax.all_to_all(pieces, ("x", "yh"), 0, 0)
    tiles = received[:, 144:]
    codes = tiles[:, :, :32].astype(F32)
    lists = (codes[:, :, :16] * 64 + codes[:, :, 16:]).astype(jnp.int32).reshape(64, 16)

    near = [received[:, :144]]
    sib = [swap(near[0])]
    own_tile, sib_tile = tiles[0], swap(tiles[0])
    for _ in range(3):
        near.append(ring(near[-1]))
        sib.append(ring(sib[-1]))
    near.append(ring(near[-1]))
    bins = unpack(near[0], sib[0], None, 0)
    for s in range(1, 4):
        bins = unpack(near[s], sib[s], bins, s)
        bins = unpack(swap(sib[s]), swap(near[s]), bins, 8 - s)
    bins = unpack(near[4], swap(near[4]), bins, 4)

    live = lax.dynamic_slice_in_dim(counts[:, 0], 4 * half + 2 * core, 2)
    mask = (jnp.arange(16, dtype=jnp.int32)[None, :] < live[:, None]).astype(F32)
    rows = []
    for sub in range(2):
        partial = grams(sub, lists, own_tile, sib_tile, bins)
        parts = lax.all_to_all(partial, ("x", "yh", "yl"), 0, 0)
        summed = jnp.sum(parts.astype(F32), axis=0) / 24
        flat = summed.reshape(48, 16, 24).transpose(1, 0, 2).reshape(16, 1152)
        rows.append(flat * mask[sub][:, None])
    return lax.all_gather(jnp.stack(rows), ("yl", "core")).reshape(8, 1, 16, 1152)


def solution(mesh):
    fine = Mesh(mesh.devices.reshape(4, 2, 8, 2, 2), ("x", "yh", "z", "yl", "core"))
    freq, space = ("x", "yh", "z"), ("yl", "core")
    return jax.shard_map(
        body,
        mesh=fine,
        in_specs=(
            P(None, freq, None, None, None, space),
            P(space),
            P(None, freq, None),
            P(None, freq),
        ),
        out_specs=P(None, freq, None, None),
        check_vma=False,
    )
```

```python
import jax
import jax.numpy as jnp
from jax import lax
from jax.experimental import pallas as pl
from jax.experimental.pallas import tpu as pltpu
from jax.sharding import Mesh
from jax.sharding import PartitionSpec as P

F32, BF16 = jnp.float32, jnp.bfloat16
LANES = 128
MIB = 1024 * 1024


def split_kernel(x_ref, triads_ref, weights_ref, out_ref):
    block = lax.broadcasted_iota(jnp.int32, (24, LANES), 1) // 16
    for q in range(6):
        sources = [x_ref[8 * q + s].astype(F32) for s in range(8)]
        for piece in range(8):
            built = None
            for s in range(8):
                shift = (s - piece) % 8 * 16
                moved = pltpu.roll(sources[s], shift, 1) if shift else sources[s]
                built = moved if built is None else jnp.where(block == s, moved, built)
            out_ref[piece, 24 * q : 24 * q + 24] = built.astype(BF16)
    listed = triads_ref[...]
    rest = weights_ref[...]
    parts = []
    for _ in range(3):
        parts.append(rest.astype(BF16))
        rest = rest - parts[-1].astype(F32)
    for piece in range(8):
        tile = [(listed >> 6).astype(F32), (listed & 63).astype(F32)]
        for part in parts:
            own = part[:, 16 * piece : 16 * piece + 16].astype(F32)
            tile.append(jnp.broadcast_to(own, (8, 16)))
        tile.append(jnp.zeros((8, 48), F32))
        out_ref[piece, 144:152] = jnp.concatenate(tile, axis=1).astype(BF16)


def unpack_kernel(own_ref, sib_ref, *refs):
    bins_ref = refs[-1]
    lane = lax.broadcasted_iota(jnp.int32, (24, LANES), 1)

    @pl.loop(0, 8)
    def _(column):
        tiles = [
            [ref[column, 24 * q : 24 * q + 24].astype(F32) for q in range(6)]
            for ref in (own_ref, sib_ref)
        ]
        for r in range(8):
            for part in range(2):
                q, offset = divmod(96 * r + 48 * part, LANES)
                halves = []
                for core in range(2):
                    picked = tiles[core][q]
                    if offset + 48 > LANES:
                        picked = jnp.where(lane >= offset, picked, tiles[core][q + 1])
                    shift = (48 * core - offset) % LANES
                    halves.append(pltpu.roll(picked, shift, 1) if shift else picked)
                merged = jnp.where(lane < 48, halves[0], halves[1])
                lanes = slice(LANES * part, LANES * (part + 1))
                bins_ref[column * 8 + r, :, lanes] = merged.astype(BF16)


def lane_weights(own_ref, sib_ref):
    lane = lax.broadcasted_iota(jnp.int32, (8, LANES), 1)
    total = jnp.zeros((8, LANES), F32)
    for core, ref in enumerate((own_ref, sib_ref)):
        tile = ref[...].astype(F32)
        for component in range(3):
            begin = 48 * core + 16 * component
            inside = (lane >= begin) & (lane < begin + 16)
            value = sum(pltpu.roll(tile, (begin - 32 - 16 * n) % LANES, 1) for n in range(3))
            total = jnp.where(inside, value, total)
    return total[0:1]


def grams_kernel(triads_ref, own_w_ref, sib_w_ref, bins_ref, out_ref, *scratch):
    buffers = (scratch[0:2], scratch[2:4])
    depth, core = lax.axis_index("z"), lax.axis_index("core")
    up = 1 - 2 * core

    def slot(which):
        turn = (up * (depth - (which & 7))) & 7
        return turn * 64 + (which & 56) + (which >> 6)

    weights = lane_weights(own_w_ref, sib_w_ref)
    lane = lax.broadcasted_iota(jnp.int32, (48, LANES), 1)

    def prepare(reader, buffer):
        w_ref, q_ref = buffer
        owner = reader >> 2
        row = (reader & 2) * 2 + core * 2 + (reader & 1)
        k_bin = row * 64 + owner * 8 + depth
        first = bins_ref[owner * 8 + row].astype(F32)
        k_real = first[:, :LANES] * weights
        k_imag = first[:, LANES:] * weights

        def some(triads):
            for t in triads:
                l_bin = triads_ref[owner * 8 + row, t]
                m_bin = (k_bin + l_bin) & 511
                second = bins_ref[slot(l_bin)].astype(F32)
                l_real, l_imag = second[:, :LANES], second[:, LANES:]
                real = (k_real * l_real - k_imag * l_imag).astype(BF16)
                imag = k_real * l_imag + k_imag * l_real
                plus, minus = imag.astype(BF16), (-imag).astype(BF16)
                w_ref[48 * t : 48 * t + 24, :LANES] = real
                w_ref[48 * t : 48 * t + 24, LANES:] = plus
                w_ref[48 * t + 24 : 48 * t + 48, :LANES] = minus
                w_ref[48 * t + 24 : 48 * t + 48, LANES:] = real
                q_ref[24 * t : 24 * t + 24, :] = bins_ref[slot(m_bin)]

        return some

    def multiply(reader, buffer, n):
        w_ref, q_ref = buffer
        start = 5 * n
        product = lax.dot_general(
            w_ref[48 * start : 48 * (start + 6), :],
            q_ref[LANES * n : LANES * (n + 1), :],
            (((1,), (1,)), ((), ())),
            preferred_element_type=F32,
        )
        built = product[:48]
        for i in range(1, 6):
            begin = 24 * (start + i) - LANES * n
            built = jnp.where(lane >= begin, product[48 * i : 48 * (i + 1)], built)
        lanes = slice(LANES * n, LANES * (n + 1))
        out_ref[reader >> 1, reader & 1, :, lanes] = built.astype(BF16)

    thirds = (range(0, 5), range(5, 10), range(10, 16))
    ready = prepare(0, buffers[0])
    for third in thirds:
        ready(third)

    @pl.loop(0, 16)
    def _(pair):
        for side in range(2):
            reader = 2 * pair + side
            following = prepare((reader + 1) & 31, buffers[1 - side])
            for n, third in enumerate(thirds):
                multiply(reader, buffers[side], n)
                following(third)


def vmem():
    return pl.BlockSpec(memory_space=pltpu.VMEM)


def smem():
    return pl.BlockSpec(memory_space=pltpu.SMEM)


def step(array, axes, by):
    size = lax.axis_size(axes)
    return lax.ppermute(array, axes, [(i, (i + by) % size) for i in range(size)])


def swap(array):
    return step(array, "core", 1)


def ring(array, crossed=False):
    pairs = []
    for z in range(8):
        up, down = (2 * z + 2) % 16, (2 * z - 2) % 16 + 1
        pairs += [(2 * z, down), (2 * z + 1, up)] if crossed else [(2 * z, up), (2 * z + 1, down)]
    return lax.ppermute(array, ("z", "core"), pairs)


def params(mib):
    return pltpu.CompilerParams(vmem_limit_bytes=mib * MIB)


BINS = jax.ShapeDtypeStruct((512, 24, 256), BF16)


def unpack(own, sib, bins, turn):
    operands = [own, sib] + ([] if bins is None else [bins])
    return pl.pallas_call(
        unpack_kernel,
        out_shape=BINS,
        grid=(1,),
        in_specs=[pl.BlockSpec((8, 144, LANES), lambda i: (0, 0, 0))] * 2
        + [pl.BlockSpec(memory_space=pl.ANY)] * (len(operands) - 2),
        out_specs=pl.BlockSpec((64, 24, 256), lambda i: (turn, 0, 0)),
        input_output_aliases={} if bins is None else {2: 0},
        compiler_params=params(8),
        cost_estimate=pl.CostEstimate(flops=1500000000, bytes_accessed=2000000, transcendentals=0),
        name="unpack",
    )(*operands)


def grams(lists, own_tile, sib_tile, bins):
    return pl.pallas_call(
        grams_kernel,
        out_shape=jax.ShapeDtypeStruct((16, 2, 48, 384), BF16),
        in_specs=[smem()] + [vmem()] * 3,
        out_specs=vmem(),
        scratch_shapes=[pltpu.VMEM((768, 256), BF16), pltpu.VMEM((384, 256), BF16)] * 2,
        compiler_params=params(12),
        cost_estimate=pl.CostEstimate(
            flops=12000000000, bytes_accessed=8000000, transcendentals=0
        ),
        name="grams",
    )(lists, own_tile, sib_tile, bins)


def body(modes, point_weights, triads, counts):
    core, half = lax.axis_index("core"), lax.axis_index("yl")
    pieces = pl.pallas_call(
        split_kernel,
        out_shape=jax.ShapeDtypeStruct((8, 152, LANES), BF16),
        in_specs=[vmem()] * 3,
        out_specs=vmem(),
        compiler_params=params(56),
        name="split",
    )(modes.reshape(48, 24, LANES), triads[:, 0], point_weights[None])
    received = lax.all_to_all(pieces, ("x", "yh"), 0, 0)
    codes = received[:, 144:, :32].astype(F32)
    lists = (codes[:, :, :16] * 64 + codes[:, :, 16:]).astype(jnp.int32).reshape(64, 16)

    beside = swap(received)
    near, sib = [received[:, :144]], [beside[:, :144]]
    near.append(ring(near[0]))
    sib.append(ring(near[0], crossed=True))
    for _ in range(2):
        near.append(ring(near[-1]))
        sib.append(ring(sib[-1]))
    near.append(ring(near[-1]))
    bins = unpack(near[0], sib[0], None, 0)
    passed = [(swap(sib[s]), swap(near[s])) for s in range(1, 4)]
    bins = unpack(near[1], sib[1], bins, 1)
    bins = unpack(*passed[0], bins, 7)
    bins = unpack(near[2], sib[2], bins, 2)
    bins = unpack(near[3], sib[3], bins, 3)
    bins = unpack(*passed[1], bins, 6)
    bins = unpack(*passed[2], bins, 5)
    bins = unpack(near[4], swap(near[4]), bins, 4)

    live = lax.dynamic_slice_in_dim(counts[:, 0], 4 * half + 2 * core, 2)
    mask = (jnp.arange(16, dtype=jnp.int32)[None, :] < live[:, None]).astype(F32)
    partial = grams(lists, received[0, 144:], beside[0, 144:], bins)
    parts = lax.all_to_all(partial, ("x", "yh", "yl"), 0, 0)
    summed = jnp.sum(parts.astype(F32), axis=0) / 24
    rows = summed.reshape(2, 48, 16, 24).transpose(0, 2, 1, 3).reshape(2, 16, 1152)
    rows = rows * mask[:, :, None]
    return lax.all_gather(rows, ("yl", "core")).reshape(8, 1, 16, 1152)


def solution(mesh):
    fine = Mesh(mesh.devices.reshape(4, 2, 8, 2, 2), ("x", "yh", "z", "yl", "core"))
    freq, space = ("x", "yh", "z"), ("yl", "core")
    return jax.shard_map(
        body,
        mesh=fine,
        in_specs=(
            P(None, freq, None, None, None, space),
            P(space),
            P(None, freq, None),
            P(None, freq),
        ),
        out_specs=P(None, freq, None, None),
        check_vma=False,
    )
```

```python
import jax
import jax.numpy as jnp
from jax import lax
from jax.experimental import pallas as pl
from jax.experimental.pallas import tpu as pltpu
from jax.sharding import Mesh
from jax.sharding import PartitionSpec as P

F32, BF16 = jnp.float32, jnp.bfloat16
LANES = 128
MIB = 1024 * 1024


def split_kernel(x_ref, triads_ref, weights_ref, out_ref):
    block = lax.broadcasted_iota(jnp.int32, (24, LANES), 1) // 16
    for q in range(6):
        sources = [x_ref[8 * q + s].astype(F32) for s in range(8)]
        for piece in range(8):
            built = None
            for s in range(8):
                shift = (s - piece) % 8 * 16
                moved = pltpu.roll(sources[s], shift, 1) if shift else sources[s]
                built = moved if built is None else jnp.where(block == s, moved, built)
            out_ref[piece, 24 * q : 24 * q + 24] = built.astype(BF16)
    listed = triads_ref[...]
    rest = weights_ref[...]
    parts = []
    for _ in range(3):
        parts.append(rest.astype(BF16))
        rest = rest - parts[-1].astype(F32)
    for piece in range(8):
        tile = [(listed >> 6).astype(F32), (listed & 63).astype(F32)]
        for part in parts:
            own = part[:, 16 * piece : 16 * piece + 16].astype(F32)
            tile.append(jnp.broadcast_to(own, (8, 16)))
        tile.append(jnp.zeros((8, 48), F32))
        out_ref[piece, 144:152] = jnp.concatenate(tile, axis=1).astype(BF16)


def unpack_kernel(own_ref, sib_ref, *refs):
    bins_ref = refs[-1]
    lane = lax.broadcasted_iota(jnp.int32, (24, LANES), 1)

    @pl.loop(0, 8)
    def _(column):
        tiles = [
            [ref[column, 24 * q : 24 * q + 24].astype(F32) for q in range(6)]
            for ref in (own_ref, sib_ref)
        ]
        for r in range(8):
            for part in range(2):
                q, offset = divmod(96 * r + 48 * part, LANES)
                halves = []
                for core in range(2):
                    picked = tiles[core][q]
                    if offset + 48 > LANES:
                        picked = jnp.where(lane >= offset, picked, tiles[core][q + 1])
                    shift = (48 * core - offset) % LANES
                    halves.append(pltpu.roll(picked, shift, 1) if shift else picked)
                merged = jnp.where(lane < 48, halves[0], halves[1])
                lanes = slice(LANES * part, LANES * (part + 1))
                bins_ref[column * 8 + r, :, lanes] = merged.astype(BF16)


def lane_weights(own_ref, sib_ref):
    lane = lax.broadcasted_iota(jnp.int32, (8, LANES), 1)
    total = jnp.zeros((8, LANES), F32)
    for core, ref in enumerate((own_ref, sib_ref)):
        tile = ref[...].astype(F32)
        for component in range(3):
            begin = 48 * core + 16 * component
            inside = (lane >= begin) & (lane < begin + 16)
            value = sum(pltpu.roll(tile, (begin - 32 - 16 * n) % LANES, 1) for n in range(3))
            total = jnp.where(inside, value, total)
    return total[0:1]


def grams_kernel(triads_ref, own_w_ref, sib_w_ref, bins_ref, out_ref, *scratch):
    buffers = (scratch[0:2], scratch[2:4])
    depth, core = lax.axis_index("z"), lax.axis_index("core")
    up = 1 - 2 * core

    def slot(which):
        turn = (up * (depth - (which & 7))) & 7
        return turn * 64 + (which & 56) + (which >> 6)

    weights = lane_weights(own_w_ref, sib_w_ref)
    lane = lax.broadcasted_iota(jnp.int32, (24, LANES), 1)

    def prepare(reader, buffer):
        w_ref, q_ref = buffer
        owner = reader >> 2
        row = (reader & 2) * 2 + core * 2 + (reader & 1)
        k_bin = row * 64 + owner * 8 + depth
        first = bins_ref[owner * 8 + row].astype(F32)
        k_real = first[:, :LANES] * weights
        k_imag = first[:, LANES:] * weights

        def some(triads):
            for t in triads:
                l_bin = triads_ref[owner * 8 + row, t]
                m_bin = (k_bin + l_bin) & 511
                second = bins_ref[slot(l_bin)].astype(F32)
                l_real, l_imag = second[:, :LANES], second[:, LANES:]
                rows = slice(24 * t, 24 * t + 24)
                w_ref[rows, :LANES] = (k_real * l_real - k_imag * l_imag).astype(BF16)
                w_ref[rows, LANES:] = (k_real * l_imag + k_imag * l_real).astype(BF16)
                third = bins_ref[slot(m_bin)]
                q_ref[48 * t : 48 * t + 24, :] = third
                q_ref[48 * t + 24 : 48 * t + 48, :LANES] = third[:, LANES:]
                q_ref[48 * t + 24 : 48 * t + 48, LANES:] = -third[:, :LANES]

        return some

    def multiply(reader, buffer, n):
        w_ref, q_ref = buffer
        start = 5 * n
        product = lax.dot_general(
            w_ref[24 * start : 24 * (start + 6), :],
            q_ref[256 * n : 256 * (n + 1), :],
            (((1,), (1,)), ((), ())),
            preferred_element_type=F32,
        )
        for side in range(2):
            first_lane = 256 * n + LANES * side
            lanes = slice(LANES * side, LANES * (side + 1))
            built = None
            for i in range(6):
                begin = 48 * (start + i) - first_lane
                if begin < LANES and begin + 48 > 0:
                    part = product[24 * i : 24 * (i + 1), lanes]
                    built = part if built is None else jnp.where(lane >= begin, part, built)
            where = slice(first_lane, first_lane + LANES)
            out_ref[reader >> 1, reader & 1, :, where] = built.astype(BF16)

    thirds = (range(0, 5), range(5, 10), range(10, 16))
    ready = prepare(0, buffers[0])
    for third in thirds:
        ready(third)

    @pl.loop(0, 16)
    def _(pair):
        for side in range(2):
            reader = 2 * pair + side
            following = prepare((reader + 1) & 31, buffers[1 - side])
            for n, third in enumerate(thirds):
                multiply(reader, buffers[side], n)
                following(third)


def vmem():
    return pl.BlockSpec(memory_space=pltpu.VMEM)


def smem():
    return pl.BlockSpec(memory_space=pltpu.SMEM)


def step(array, axes, by):
    size = lax.axis_size(axes)
    return lax.ppermute(array, axes, [(i, (i + by) % size) for i in range(size)])


def swap(array):
    return step(array, "core", 1)


def ring(array, crossed=False):
    pairs = []
    for z in range(8):
        up, down = (2 * z + 2) % 16, (2 * z - 2) % 16 + 1
        pairs += [(2 * z, down), (2 * z + 1, up)] if crossed else [(2 * z, up), (2 * z + 1, down)]
    return lax.ppermute(array, ("z", "core"), pairs)


def params(mib):
    return pltpu.CompilerParams(vmem_limit_bytes=mib * MIB)


BINS = jax.ShapeDtypeStruct((512, 24, 256), BF16)


def unpack(own, sib, bins, turn):
    operands = [own, sib] + ([] if bins is None else [bins])
    return pl.pallas_call(
        unpack_kernel,
        out_shape=BINS,
        grid=(1,),
        in_specs=[pl.BlockSpec((8, 144, LANES), lambda i: (0, 0, 0))] * 2
        + [pl.BlockSpec(memory_space=pl.ANY)] * (len(operands) - 2),
        out_specs=pl.BlockSpec((64, 24, 256), lambda i: (turn, 0, 0)),
        input_output_aliases={} if bins is None else {2: 0},
        compiler_params=params(8),
        cost_estimate=pl.CostEstimate(flops=3000000000, bytes_accessed=2000000, transcendentals=0),
        name="unpack",
    )(*operands)


def grams(lists, own_tile, sib_tile, bins):
    return pl.pallas_call(
        grams_kernel,
        out_shape=jax.ShapeDtypeStruct((16, 2, 24, 768), BF16),
        in_specs=[smem()] + [vmem()] * 3,
        out_specs=vmem(),
        scratch_shapes=[pltpu.VMEM((384, 256), BF16), pltpu.VMEM((768, 256), BF16)] * 2,
        compiler_params=params(12),
        cost_estimate=pl.CostEstimate(
            flops=12000000000, bytes_accessed=8000000, transcendentals=0
        ),
        name="grams",
    )(lists, own_tile, sib_tile, bins)


def body(modes, point_weights, triads, counts):
    core, half = lax.axis_index("core"), lax.axis_index("yl")
    pieces = pl.pallas_call(
        split_kernel,
        out_shape=jax.ShapeDtypeStruct((8, 152, LANES), BF16),
        in_specs=[vmem()] * 3,
        out_specs=vmem(),
        compiler_params=params(56),
        name="split",
    )(modes.reshape(48, 24, LANES), triads[:, 0], point_weights[None])
    received = lax.all_to_all(pieces, ("x", "yh"), 0, 0)
    codes = received[:, 144:, :32].astype(F32)
    lists = (codes[:, :, :16] * 64 + codes[:, :, 16:]).astype(jnp.int32).reshape(64, 16)

    beside = swap(received)
    near, sib = [received[:, :144]], [beside[:, :144]]
    near.append(ring(near[0]))
    sib.append(ring(near[0], crossed=True))
    for _ in range(2):
        near.append(ring(near[-1]))
        sib.append(ring(sib[-1]))
    near.append(ring(near[-1]))
    bins = unpack(near[0], sib[0], None, 0)
    passed = [(swap(sib[s]), swap(near[s])) for s in range(1, 4)]
    bins = unpack(near[1], sib[1], bins, 1)
    bins = unpack(*passed[0], bins, 7)
    bins = unpack(near[2], sib[2], bins, 2)
    bins = unpack(near[3], sib[3], bins, 3)
    bins = unpack(*passed[1], bins, 6)
    bins = unpack(*passed[2], bins, 5)
    bins = unpack(near[4], swap(near[4]), bins, 4)

    live = lax.dynamic_slice_in_dim(counts[:, 0], 4 * half + 2 * core, 2)
    mask = (jnp.arange(16, dtype=jnp.int32)[None, :] < live[:, None]).astype(F32)
    partial = grams(lists, received[0, 144:], beside[0, 144:], bins)
    parts = lax.all_to_all(partial, ("x", "yh", "yl"), 0, 0)
    summed = jnp.sum(parts.astype(F32), axis=0) / 24
    rows = summed.reshape(2, 24, 16, 2, 24).transpose(0, 2, 3, 1, 4).reshape(2, 1, 16, 1152)
    rows = rows * mask[:, None, :, None]
    return lax.all_gather(rows, ("yl", "core"), tiled=True)


def solution(mesh):
    fine = Mesh(mesh.devices.reshape(4, 2, 8, 2, 2), ("x", "yh", "z", "yl", "core"))
    freq, space = ("x", "yh", "z"), ("yl", "core")
    return jax.shard_map(
        body,
        mesh=fine,
        in_specs=(
            P(None, freq, None, None, None, space),
            P(space),
            P(None, freq, None),
            P(None, freq),
        ),
        out_specs=P(None, freq, None, None),
        check_vma=False,
    )
```

```python
import jax
import jax.numpy as jnp
from jax import lax
from jax.experimental import pallas as pl
from jax.experimental.pallas import tpu as pltpu
from jax.sharding import Mesh
from jax.sharding import PartitionSpec as P

F32, BF16 = jnp.float32, jnp.bfloat16
LANES = 128
MIB = 1024 * 1024


def split_kernel(x_ref, triads_ref, weights_ref, out_ref):
    block = lax.broadcasted_iota(jnp.int32, (24, LANES), 1) // 16
    for q in range(6):
        sources = [x_ref[8 * q + s].astype(F32) for s in range(8)]
        for piece in range(8):
            built = None
            for s in range(8):
                shift = (s - piece) % 8 * 16
                moved = pltpu.roll(sources[s], shift, 1) if shift else sources[s]
                built = moved if built is None else jnp.where(block == s, moved, built)
            out_ref[piece, 24 * q : 24 * q + 24] = built.astype(BF16)
    listed = triads_ref[...]
    rest = weights_ref[...]
    parts = []
    for _ in range(3):
        parts.append(rest.astype(BF16))
        rest = rest - parts[-1].astype(F32)
    for piece in range(8):
        tile = [(listed >> 6).astype(F32), (listed & 63).astype(F32)]
        for part in parts:
            own = part[:, 16 * piece : 16 * piece + 16].astype(F32)
            tile.append(jnp.broadcast_to(own, (8, 16)))
        tile.append(jnp.zeros((8, 48), F32))
        out_ref[piece, 144:152] = jnp.concatenate(tile, axis=1).astype(BF16)


def unpack_kernel(own_ref, sib_ref, *refs):
    bins_ref = refs[-1]
    lane = lax.broadcasted_iota(jnp.int32, (24, LANES), 1)

    @pl.loop(0, 8)
    def _(column):
        tiles = [
            [ref[column, 24 * q : 24 * q + 24].astype(F32) for q in range(6)]
            for ref in (own_ref, sib_ref)
        ]
        for r in range(8):
            for part in range(2):
                q, offset = divmod(96 * r + 48 * part, LANES)
                halves = []
                for core in range(2):
                    picked = tiles[core][q]
                    if offset + 48 > LANES:
                        picked = jnp.where(lane >= offset, picked, tiles[core][q + 1])
                    shift = (48 * core - offset) % LANES
                    halves.append(pltpu.roll(picked, shift, 1) if shift else picked)
                merged = jnp.where(lane < 48, halves[0], halves[1])
                lanes = slice(LANES * part, LANES * (part + 1))
                bins_ref[column * 8 + r, :, lanes] = merged.astype(BF16)


def lane_weights(own_ref, sib_ref):
    lane = lax.broadcasted_iota(jnp.int32, (8, LANES), 1)
    total = jnp.zeros((8, LANES), F32)
    for core, ref in enumerate((own_ref, sib_ref)):
        tile = ref[...].astype(F32)
        for component in range(3):
            begin = 48 * core + 16 * component
            inside = (lane >= begin) & (lane < begin + 16)
            value = sum(pltpu.roll(tile, (begin - 32 - 16 * n) % LANES, 1) for n in range(3))
            total = jnp.where(inside, value, total)
    return total[0:1]


def grams_kernel(triads_ref, own_w_ref, sib_w_ref, bins_ref, out_ref, *scratch):
    buffers = (scratch[0:2], scratch[2:4])
    depth, core = lax.axis_index("z"), lax.axis_index("core")
    up = 1 - 2 * core

    def slot(which):
        turn = (up * (depth - (which & 7))) & 7
        return turn * 64 + (which & 56) + (which >> 6)

    weights = lane_weights(own_w_ref, sib_w_ref)
    lane = lax.broadcasted_iota(jnp.int32, (48, LANES), 1)

    def prepare(reader, buffer):
        w_ref, q_ref = buffer
        owner = reader >> 2
        row = (reader & 2) * 2 + core * 2 + (reader & 1)
        k_bin = row * 64 + owner * 8 + depth
        first = bins_ref[owner * 8 + row].astype(F32)
        k_real = first[:, :LANES] * weights
        k_imag = first[:, LANES:] * weights

        def some(triads):
            for t in triads:
                l_bin = triads_ref[owner * 8 + row, t]
                m_bin = (k_bin + l_bin) & 511
                second = bins_ref[slot(l_bin)].astype(F32)
                l_real, l_imag = second[:, :LANES], second[:, LANES:]
                real = (k_real * l_real - k_imag * l_imag).astype(BF16)
                imag = k_real * l_imag + k_imag * l_real
                plus, minus = imag.astype(BF16), (-imag).astype(BF16)
                w_ref[48 * t : 48 * t + 24, :LANES] = real
                w_ref[48 * t : 48 * t + 24, LANES:] = plus
                w_ref[48 * t + 24 : 48 * t + 48, :LANES] = minus
                w_ref[48 * t + 24 : 48 * t + 48, LANES:] = real
                q_ref[24 * t : 24 * t + 24, :] = bins_ref[slot(m_bin)]

        return some

    def multiply(reader, buffer, n):
        w_ref, q_ref = buffer
        start = 5 * n
        product = lax.dot_general(
            w_ref[48 * start : 48 * (start + 6), :],
            q_ref[LANES * n : LANES * (n + 1), :],
            (((1,), (1,)), ((), ())),
            preferred_element_type=F32,
        )
        built = product[:48]
        for i in range(1, 6):
            begin = 24 * (start + i) - LANES * n
            built = jnp.where(lane >= begin, product[48 * i : 48 * (i + 1)], built)
        lanes = slice(LANES * n, LANES * (n + 1))
        out_ref[reader >> 1, reader & 1, :, lanes] = built.astype(BF16)

    thirds = (range(0, 5), range(5, 10), range(10, 16))
    ready = prepare(0, buffers[0])
    for third in thirds:
        ready(third)

    @pl.loop(0, 16, unroll=2)
    def _(pair):
        for side in range(2):
            reader = 2 * pair + side
            following = prepare((reader + 1) & 31, buffers[1 - side])
            for n, third in enumerate(thirds):
                multiply(reader, buffers[side], n)
                following(third)


def vmem():
    return pl.BlockSpec(memory_space=pltpu.VMEM)


def smem():
    return pl.BlockSpec(memory_space=pltpu.SMEM)


def step(array, axes, by):
    size = lax.axis_size(axes)
    return lax.ppermute(array, axes, [(i, (i + by) % size) for i in range(size)])


def swap(array):
    return step(array, "core", 1)


def ring(array, crossed=False):
    pairs = []
    for z in range(8):
        up, down = (2 * z + 2) % 16, (2 * z - 2) % 16 + 1
        pairs += [(2 * z, down), (2 * z + 1, up)] if crossed else [(2 * z, up), (2 * z + 1, down)]
    return lax.ppermute(array, ("z", "core"), pairs)


def params(mib):
    return pltpu.CompilerParams(vmem_limit_bytes=mib * MIB)


BINS = jax.ShapeDtypeStruct((512, 24, 256), BF16)


def unpack(own, sib, bins, turn):
    operands = [own, sib] + ([] if bins is None else [bins])
    return pl.pallas_call(
        unpack_kernel,
        out_shape=BINS,
        grid=(1,),
        in_specs=[pl.BlockSpec((8, 144, LANES), lambda i: (0, 0, 0))] * 2
        + [pl.BlockSpec(memory_space=pl.ANY)] * (len(operands) - 2),
        out_specs=pl.BlockSpec((64, 24, 256), lambda i: (turn, 0, 0)),
        input_output_aliases={} if bins is None else {2: 0},
        compiler_params=params(8),
        cost_estimate=pl.CostEstimate(flops=3000000000, bytes_accessed=2000000, transcendentals=0),
        name="unpack",
    )(*operands)


def grams(lists, own_tile, sib_tile, bins):
    return pl.pallas_call(
        grams_kernel,
        out_shape=jax.ShapeDtypeStruct((16, 2, 48, 384), BF16),
        in_specs=[smem()] + [vmem()] * 3,
        out_specs=vmem(),
        scratch_shapes=[pltpu.VMEM((768, 256), BF16), pltpu.VMEM((384, 256), BF16)] * 2,
        compiler_params=params(12),
        cost_estimate=pl.CostEstimate(
            flops=12000000000, bytes_accessed=8000000, transcendentals=0
        ),
        name="grams",
    )(lists, own_tile, sib_tile, bins)


def body(modes, point_weights, triads, counts):
    pieces = pl.pallas_call(
        split_kernel,
        out_shape=jax.ShapeDtypeStruct((8, 152, LANES), BF16),
        in_specs=[vmem()] * 3,
        out_specs=vmem(),
        compiler_params=params(56),
        name="split",
    )(modes.reshape(48, 24, LANES), triads[:, 0], point_weights[None])
    received = lax.all_to_all(pieces, ("x", "yh"), 0, 0)
    codes = received[:, 144:, :32].astype(F32)
    lists = (codes[:, :, :16] * 64 + codes[:, :, 16:]).astype(jnp.int32).reshape(64, 16)

    beside = swap(received)
    near, sib = [received[:, :144]], [beside[:, :144]]
    near.append(ring(near[0]))
    sib.append(ring(near[0], crossed=True))
    for _ in range(2):
        near.append(ring(near[-1]))
        sib.append(ring(sib[-1]))
    near.append(ring(near[-1]))
    bins = unpack(near[0], sib[0], None, 0)
    passed = [(swap(sib[s]), swap(near[s])) for s in range(1, 4)]
    bins = unpack(near[1], sib[1], bins, 1)
    bins = unpack(*passed[0], bins, 7)
    bins = unpack(near[2], sib[2], bins, 2)
    bins = unpack(near[3], sib[3], bins, 3)
    bins = unpack(*passed[1], bins, 6)
    bins = unpack(*passed[2], bins, 5)
    bins = unpack(near[4], swap(near[4]), bins, 4)

    partial = grams(lists, received[0, 144:], beside[0, 144:], bins)
    parts = lax.all_to_all(partial, ("x", "yh", "yl"), 0, 0)
    summed = jnp.sum(parts.astype(F32), axis=0) / 24
    rows = summed.reshape(2, 48, 16, 24).transpose(0, 2, 1, 3).reshape(2, 1, 16, 1152)
    gathered = lax.all_gather(rows, ("yl", "core"), tiled=True)
    live = jnp.arange(16, dtype=jnp.int32)[None, None, :, None] < counts[:, :, None, None]
    return jnp.where(live, gathered, 0.0)


def solution(mesh):
    fine = Mesh(mesh.devices.reshape(4, 2, 8, 2, 2), ("x", "yh", "z", "yl", "core"))
    freq, space = ("x", "yh", "z"), ("yl", "core")
    return jax.shard_map(
        body,
        mesh=fine,
        in_specs=(
            P(None, freq, None, None, None, space),
            P(space),
            P(None, freq, None),
            P(None, freq),
        ),
        out_specs=P(None, freq, None, None),
        check_vma=False,
    )
```

```python
import jax
import jax.numpy as jnp
from jax import lax
from jax.experimental import pallas as pl
from jax.experimental.pallas import tpu as pltpu
from jax.sharding import Mesh
from jax.sharding import PartitionSpec as P

F32, BF16 = jnp.float32, jnp.bfloat16
LANES = 128
MIB = 1024 * 1024


def split_kernel(x_ref, triads_ref, weights_ref, out_ref):
    block = lax.broadcasted_iota(jnp.int32, (24, LANES), 1) // 16
    for q in range(6):
        sources = [x_ref[8 * q + s].astype(F32) for s in range(8)]
        for piece in range(8):
            built = None
            for s in range(8):
                shift = (s - piece) % 8 * 16
                moved = pltpu.roll(sources[s], shift, 1) if shift else sources[s]
                built = moved if built is None else jnp.where(block == s, moved, built)
            out_ref[piece, 24 * q : 24 * q + 24] = built.astype(BF16)
    listed = triads_ref[...]
    rest = weights_ref[...]
    parts = []
    for _ in range(3):
        parts.append(rest.astype(BF16))
        rest = rest - parts[-1].astype(F32)
    for piece in range(8):
        tile = [(listed >> 6).astype(F32), (listed & 63).astype(F32)]
        for part in parts:
            own = part[:, 16 * piece : 16 * piece + 16].astype(F32)
            tile.append(jnp.broadcast_to(own, (8, 16)))
        tile.append(jnp.zeros((8, 48), F32))
        out_ref[piece, 144:152] = jnp.concatenate(tile, axis=1).astype(BF16)


def unpack_kernel(own_ref, sib_ref, *refs):
    bins_ref = refs[-1]
    lane = lax.broadcasted_iota(jnp.int32, (24, LANES), 1)

    @pl.loop(0, 8)
    def _(column):
        tiles = [
            [ref[column, 24 * q : 24 * q + 24].astype(F32) for q in range(6)]
            for ref in (own_ref, sib_ref)
        ]
        for r in range(8):
            for part in range(2):
                q, offset = divmod(96 * r + 48 * part, LANES)
                halves = []
                for core in range(2):
                    picked = tiles[core][q]
                    if offset + 48 > LANES:
                        picked = jnp.where(lane >= offset, picked, tiles[core][q + 1])
                    shift = (48 * core - offset) % LANES
                    halves.append(pltpu.roll(picked, shift, 1) if shift else picked)
                merged = jnp.where(lane < 48, halves[0], halves[1])
                lanes = slice(LANES * part, LANES * (part + 1))
                bins_ref[column * 8 + r, :, lanes] = merged.astype(BF16)


def lane_weights(own_ref, sib_ref):
    lane = lax.broadcasted_iota(jnp.int32, (8, LANES), 1)
    total = jnp.zeros((8, LANES), F32)
    for core, ref in enumerate((own_ref, sib_ref)):
        tile = ref[...].astype(F32)
        for component in range(3):
            begin = 48 * core + 16 * component
            inside = (lane >= begin) & (lane < begin + 16)
            value = sum(pltpu.roll(tile, (begin - 32 - 16 * n) % LANES, 1) for n in range(3))
            total = jnp.where(inside, value, total)
    return total[0:1]


def grams_kernel(triads_ref, own_w_ref, sib_w_ref, bins_ref, out_ref, *scratch):
    buffers = (scratch[0:2], scratch[2:4])
    depth, core = lax.axis_index("z"), lax.axis_index("core")
    up = 1 - 2 * core

    def slot(which):
        turn = (up * (depth - (which & 7))) & 7
        return turn * 64 + (which & 56) + (which >> 6)

    weights = lane_weights(own_w_ref, sib_w_ref)
    lane = lax.broadcasted_iota(jnp.int32, (48, LANES), 1)

    def prepare(reader, buffer):
        w_ref, q_ref = buffer
        owner = reader >> 2
        row = (reader & 2) * 2 + core * 2 + (reader & 1)
        k_bin = row * 64 + owner * 8 + depth
        first = bins_ref[owner * 8 + row].astype(F32)
        k_real = first[:, :LANES] * weights
        k_imag = first[:, LANES:] * weights

        def some(triads):
            for t in triads:
                l_bin = triads_ref[owner * 8 + row, t]
                m_bin = (k_bin + l_bin) & 511
                second = bins_ref[slot(l_bin)].astype(F32)
                l_real, l_imag = second[:, :LANES], second[:, LANES:]
                real = (k_real * l_real - k_imag * l_imag).astype(BF16)
                imag = k_real * l_imag + k_imag * l_real
                plus, minus = imag.astype(BF16), (-imag).astype(BF16)
                w_ref[48 * t : 48 * t + 24, :LANES] = real
                w_ref[48 * t : 48 * t + 24, LANES:] = plus
                w_ref[48 * t + 24 : 48 * t + 48, :LANES] = minus
                w_ref[48 * t + 24 : 48 * t + 48, LANES:] = real
                q_ref[24 * t : 24 * t + 24, :] = bins_ref[slot(m_bin)]

        return some

    def multiply(reader, buffer, n):
        w_ref, q_ref = buffer
        start = 5 * n
        product = lax.dot_general(
            w_ref[48 * start : 48 * (start + 6), :],
            q_ref[LANES * n : LANES * (n + 1), :],
            (((1,), (1,)), ((), ())),
            preferred_element_type=F32,
        )
        built = product[:48]
        for i in range(1, 6):
            begin = 24 * (start + i) - LANES * n
            built = jnp.where(lane >= begin, product[48 * i : 48 * (i + 1)], built)
        lanes = slice(LANES * n, LANES * (n + 1))
        out_ref[reader >> 1, reader & 1, :, lanes] = built.astype(BF16)

    thirds = (range(0, 5), range(5, 10), range(10, 16))
    ready = prepare(0, buffers[0])
    for third in thirds:
        ready(third)

    @pl.loop(0, 16, unroll=2)
    def _(pair):
        for side in range(2):
            reader = 2 * pair + side
            following = prepare((reader + 1) & 31, buffers[1 - side])
            for n, third in enumerate(thirds):
                multiply(reader, buffers[side], n)
                following(third)


def vmem():
    return pl.BlockSpec(memory_space=pltpu.VMEM)


def smem():
    return pl.BlockSpec(memory_space=pltpu.SMEM)


def step(array, axes, by):
    size = lax.axis_size(axes)
    return lax.ppermute(array, axes, [(i, (i + by) % size) for i in range(size)])


def swap(array):
    return step(array, "core", 1)


def ring(array, crossed=False):
    pairs = []
    for z in range(8):
        up, down = (2 * z + 2) % 16, (2 * z - 2) % 16 + 1
        pairs += [(2 * z, down), (2 * z + 1, up)] if crossed else [(2 * z, up), (2 * z + 1, down)]
    return lax.ppermute(array, ("z", "core"), pairs)


def params(mib):
    return pltpu.CompilerParams(vmem_limit_bytes=mib * MIB)


BINS = jax.ShapeDtypeStruct((512, 24, 256), BF16)


def unpack(own, sib, bins, turn):
    operands = [own, sib] + ([] if bins is None else [bins])
    return pl.pallas_call(
        unpack_kernel,
        out_shape=BINS,
        grid=(1,),
        in_specs=[pl.BlockSpec((8, 144, LANES), lambda i: (0, 0, 0))] * 2
        + [pl.BlockSpec(memory_space=pl.ANY)] * (len(operands) - 2),
        out_specs=pl.BlockSpec((64, 24, 256), lambda i: (turn, 0, 0)),
        input_output_aliases={} if bins is None else {2: 0},
        compiler_params=params(8),
        cost_estimate=pl.CostEstimate(flops=1500000000, bytes_accessed=2000000, transcendentals=0),
        name="unpack",
    )(*operands)


def grams(lists, own_tile, sib_tile, bins):
    return pl.pallas_call(
        grams_kernel,
        out_shape=jax.ShapeDtypeStruct((16, 2, 48, 384), BF16),
        in_specs=[smem()] + [vmem()] * 3,
        out_specs=vmem(),
        scratch_shapes=[pltpu.VMEM((768, 256), BF16), pltpu.VMEM((384, 256), BF16)] * 2,
        compiler_params=params(12),
        cost_estimate=pl.CostEstimate(
            flops=12000000000, bytes_accessed=8000000, transcendentals=0
        ),
        name="grams",
    )(lists, own_tile, sib_tile, bins)


def body(modes, point_weights, triads, counts):
    pieces = pl.pallas_call(
        split_kernel,
        out_shape=jax.ShapeDtypeStruct((8, 152, LANES), BF16),
        in_specs=[vmem()] * 3,
        out_specs=vmem(),
        compiler_params=params(56),
        name="split",
    )(modes.reshape(48, 24, LANES), triads[:, 0], point_weights[None])
    received = lax.all_to_all(pieces, ("x", "yh"), 0, 0)
    codes = received[:, 144:, :32].astype(F32)
    lists = (codes[:, :, :16] * 64 + codes[:, :, 16:]).astype(jnp.int32).reshape(64, 16)

    beside = swap(received)
    near, sib = [received[:, :144]], [beside[:, :144]]
    near.append(ring(near[0]))
    sib.append(ring(near[0], crossed=True))
    for _ in range(2):
        near.append(ring(near[-1]))
        sib.append(ring(sib[-1]))
    near.append(ring(near[-1]))
    bins = unpack(near[0], sib[0], None, 0)
    passed = []
    for s in range(1, 4):
        pair = lax.optimization_barrier((sib[s], near[s]))
        passed.append((swap(pair[0]), swap(pair[1])))
    bins = unpack(near[1], sib[1], bins, 1)
    bins = unpack(*passed[0], bins, 7)
    bins = unpack(near[2], sib[2], bins, 2)
    bins = unpack(*passed[1], bins, 6)
    bins = unpack(near[3], sib[3], bins, 3)
    last, bins = lax.optimization_barrier((near[4], bins))
    last_passed = swap(last)
    bins = unpack(*passed[2], bins, 5)
    bins = unpack(last, last_passed, bins, 4)

    partial = grams(lists, received[0, 144:], beside[0, 144:], bins)
    parts = lax.all_to_all(partial, ("x", "yh", "yl"), 0, 0)
    summed = jnp.sum(parts.astype(F32), axis=0) / 24
    rows = summed.reshape(2, 48, 16, 24).transpose(0, 2, 1, 3).reshape(2, 1, 16, 1152)
    gathered = lax.all_gather(rows, ("yl", "core"), tiled=True)
    live = jnp.arange(16, dtype=jnp.int32)[None, None, :, None] < counts[:, :, None, None]
    return jnp.where(live, gathered, 0.0)


def solution(mesh):
    fine = Mesh(mesh.devices.reshape(4, 2, 8, 2, 2), ("x", "yh", "z", "yl", "core"))
    freq, space = ("x", "yh", "z"), ("yl", "core")
    return jax.shard_map(
        body,
        mesh=fine,
        in_specs=(
            P(None, freq, None, None, None, space),
            P(space),
            P(None, freq, None),
            P(None, freq),
        ),
        out_specs=P(None, freq, None, None),
        check_vma=False,
    )
```

```python
import jax
import jax.numpy as jnp
from jax import lax
from jax.experimental import pallas as pl
from jax.experimental.pallas import tpu as pltpu
from jax.sharding import Mesh
from jax.sharding import PartitionSpec as P

F32, BF16 = jnp.float32, jnp.bfloat16
LANES = 128
MIB = 1024 * 1024


def split_kernel(x_ref, triads_ref, weights_ref, out_ref):
    block = lax.broadcasted_iota(jnp.int32, (24, LANES), 1) // 16
    for q in range(6):
        sources = [x_ref[8 * q + s].astype(F32) for s in range(8)]
        for piece in range(8):
            built = None
            for s in range(8):
                shift = (s - piece) % 8 * 16
                moved = pltpu.roll(sources[s], shift, 1) if shift else sources[s]
                built = moved if built is None else jnp.where(block == s, moved, built)
            out_ref[piece, 24 * q : 24 * q + 24] = built.astype(BF16)
    listed = triads_ref[...]
    rest = weights_ref[...]
    parts = []
    for _ in range(3):
        parts.append(rest.astype(BF16))
        rest = rest - parts[-1].astype(F32)
    for piece in range(8):
        tile = [(listed >> 6).astype(F32), (listed & 63).astype(F32)]
        for part in parts:
            own = part[:, 16 * piece : 16 * piece + 16].astype(F32)
            tile.append(jnp.broadcast_to(own, (8, 16)))
        tile.append(jnp.zeros((8, 48), F32))
        out_ref[piece, 144:152] = jnp.concatenate(tile, axis=1).astype(BF16)


def unpack_kernel(own_ref, sib_ref, *refs):
    bins_ref = refs[-1]
    lane = lax.broadcasted_iota(jnp.int32, (24, LANES), 1)

    @pl.loop(0, 8)
    def _(column):
        tiles = [
            [ref[column, 24 * q : 24 * q + 24].astype(F32) for q in range(6)]
            for ref in (own_ref, sib_ref)
        ]
        for r in range(8):
            for part in range(2):
                q, offset = divmod(96 * r + 48 * part, LANES)
                halves = []
                for core in range(2):
                    picked = tiles[core][q]
                    if offset + 48 > LANES:
                        picked = jnp.where(lane >= offset, picked, tiles[core][q + 1])
                    shift = (48 * core - offset) % LANES
                    halves.append(pltpu.roll(picked, shift, 1) if shift else picked)
                merged = jnp.where(lane < 48, halves[0], halves[1])
                lanes = slice(LANES * part, LANES * (part + 1))
                bins_ref[column * 8 + r, :, lanes] = merged.astype(BF16)


def lane_weights(own_ref, sib_ref):
    lane = lax.broadcasted_iota(jnp.int32, (8, LANES), 1)
    total = jnp.zeros((8, LANES), F32)
    for core, ref in enumerate((own_ref, sib_ref)):
        tile = ref[...].astype(F32)
        for component in range(3):
            begin = 48 * core + 16 * component
            inside = (lane >= begin) & (lane < begin + 16)
            value = sum(pltpu.roll(tile, (begin - 32 - 16 * n) % LANES, 1) for n in range(3))
            total = jnp.where(inside, value, total)
    return total[0:1]


def grams_kernel(triads_ref, own_w_ref, sib_w_ref, bins_ref, out_ref, *scratch):
    buffers = (scratch[0:2], scratch[2:4])
    depth, core = lax.axis_index("z"), lax.axis_index("core")
    up = 1 - 2 * core

    def slot(which):
        turn = (up * (depth - (which & 7))) & 7
        return turn * 64 + (which & 56) + (which >> 6)

    weights = lane_weights(own_w_ref, sib_w_ref)
    lane = lax.broadcasted_iota(jnp.int32, (48, LANES), 1)

    def prepare(reader, buffer):
        w_ref, q_ref = buffer
        owner = reader >> 2
        row = (reader & 2) * 2 + core * 2 + (reader & 1)
        k_bin = row * 64 + owner * 8 + depth
        first = bins_ref[owner * 8 + row].astype(F32)
        k_real = first[:, :LANES] * weights
        k_imag = first[:, LANES:] * weights

        def some(triads):
            for t in triads:
                l_bin = triads_ref[owner * 8 + row, t]
                m_bin = (k_bin + l_bin) & 511
                second = bins_ref[slot(l_bin)].astype(F32)
                l_real, l_imag = second[:, :LANES], second[:, LANES:]
                real = (k_real * l_real - k_imag * l_imag).astype(BF16)
                imag = k_real * l_imag + k_imag * l_real
                plus, minus = imag.astype(BF16), (-imag).astype(BF16)
                w_ref[48 * t : 48 * t + 24, :LANES] = real
                w_ref[48 * t : 48 * t + 24, LANES:] = plus
                w_ref[48 * t + 24 : 48 * t + 48, :LANES] = minus
                w_ref[48 * t + 24 : 48 * t + 48, LANES:] = real
                q_ref[24 * t : 24 * t + 24, :] = bins_ref[slot(m_bin)]

        return some

    def multiply(reader, buffer, n):
        w_ref, q_ref = buffer
        start = 5 * n
        product = lax.dot_general(
            w_ref[48 * start : 48 * (start + 6), :],
            q_ref[LANES * n : LANES * (n + 1), :],
            (((1,), (1,)), ((), ())),
            preferred_element_type=F32,
        )
        built = product[:48]
        for i in range(1, 6):
            begin = 24 * (start + i) - LANES * n
            built = jnp.where(lane >= begin, product[48 * i : 48 * (i + 1)], built)
        lanes = slice(LANES * n, LANES * (n + 1))
        out_ref[reader >> 1, reader & 1, :, lanes] = built.astype(BF16)

    thirds = (range(0, 5), range(5, 10), range(10, 16))
    ready = prepare(0, buffers[0])
    for third in thirds:
        ready(third)

    @pl.loop(0, 16, unroll=2)
    def _(pair):
        for side in range(2):
            reader = 2 * pair + side
            following = prepare((reader + 1) & 31, buffers[1 - side])
            for n, third in enumerate(thirds):
                multiply(reader, buffers[side], n)
                following(third)


def vmem():
    return pl.BlockSpec(memory_space=pltpu.VMEM)


def smem():
    return pl.BlockSpec(memory_space=pltpu.SMEM)


def step(array, axes, by):
    size = lax.axis_size(axes)
    return lax.ppermute(array, axes, [(i, (i + by) % size) for i in range(size)])


def swap(array):
    return step(array, "core", 1)


def ring(array, crossed=False):
    pairs = []
    for z in range(8):
        up, down = (2 * z + 2) % 16, (2 * z - 2) % 16 + 1
        pairs += [(2 * z, down), (2 * z + 1, up)] if crossed else [(2 * z, up), (2 * z + 1, down)]
    return lax.ppermute(array, ("z", "core"), pairs)


def params(mib):
    return pltpu.CompilerParams(vmem_limit_bytes=mib * MIB)


BINS = jax.ShapeDtypeStruct((512, 24, 256), BF16)


def unpack(own, sib, bins, turn):
    operands = [own, sib] + ([] if bins is None else [bins])
    return pl.pallas_call(
        unpack_kernel,
        out_shape=BINS,
        grid=(1,),
        in_specs=[pl.BlockSpec((8, 144, LANES), lambda i: (0, 0, 0))] * 2
        + [pl.BlockSpec(memory_space=pl.ANY)] * (len(operands) - 2),
        out_specs=pl.BlockSpec((64, 24, 256), lambda i: (turn, 0, 0)),
        input_output_aliases={} if bins is None else {2: 0},
        compiler_params=params(8),
        cost_estimate=pl.CostEstimate(flops=1500000000, bytes_accessed=2000000, transcendentals=0),
        name="unpack",
    )(*operands)


def grams(lists, own_tile, sib_tile, bins):
    return pl.pallas_call(
        grams_kernel,
        out_shape=jax.ShapeDtypeStruct((16, 2, 48, 384), BF16),
        in_specs=[smem()] + [vmem()] * 3,
        out_specs=vmem(),
        scratch_shapes=[pltpu.VMEM((768, 256), BF16), pltpu.VMEM((384, 256), BF16)] * 2,
        compiler_params=params(12),
        cost_estimate=pl.CostEstimate(
            flops=12000000000, bytes_accessed=8000000, transcendentals=0
        ),
        name="grams",
    )(lists, own_tile, sib_tile, bins)


def body(modes, point_weights, triads, counts):
    pieces = pl.pallas_call(
        split_kernel,
        out_shape=jax.ShapeDtypeStruct((8, 152, LANES), BF16),
        in_specs=[vmem()] * 3,
        out_specs=vmem(),
        compiler_params=params(56),
        name="split",
    )(modes.reshape(48, 24, LANES), triads[:, 0], point_weights[None])
    received = lax.all_to_all(pieces, ("x", "yh"), 0, 0)
    codes = received[:, 144:, :32].astype(F32)
    lists = (codes[:, :, :16] * 64 + codes[:, :, 16:]).astype(jnp.int32).reshape(64, 16)

    beside = swap(received)
    near, sib = [received[:, :144]], [beside[:, :144]]
    near.append(ring(near[0]))
    sib.append(ring(near[0], crossed=True))
    for _ in range(2):
        near.append(ring(near[-1]))
        sib.append(ring(sib[-1]))
    near.append(ring(near[-1]))
    bins = unpack(near[0], sib[0], None, 0)
    passed = []
    for s in range(1, 4):
        pair = lax.optimization_barrier((sib[s], near[s]))
        passed.append((swap(pair[0]), swap(pair[1])))
    bins = unpack(near[1], sib[1], bins, 1)
    bins = unpack(*passed[0], bins, 7)
    bins = unpack(near[2], sib[2], bins, 2)
    bins = unpack(*passed[1], bins, 6)
    bins = unpack(near[3], sib[3], bins, 3)
    last, bins = lax.optimization_barrier((near[4], bins))
    last_passed = swap(last)
    bins = unpack(*passed[2], bins, 5)
    bins = unpack(last, last_passed, bins, 4)

    partial = grams(lists, received[0, 144:], beside[0, 144:], bins)
    parts = lax.all_to_all(partial, ("x", "yh", "yl"), 0, 0)
    parts, counts = lax.optimization_barrier((parts, counts))
    summed = jnp.sum(parts.astype(F32), axis=0) / 24
    rows = summed.reshape(2, 48, 16, 24).transpose(0, 2, 1, 3).reshape(2, 1, 16, 1152)
    gathered = lax.all_gather(rows, ("yl", "core"), tiled=True)
    live = jnp.arange(16, dtype=jnp.int32)[None, None, :, None] < counts[:, :, None, None]
    return jnp.where(live, gathered, 0.0)


def solution(mesh):
    fine = Mesh(mesh.devices.reshape(4, 2, 8, 2, 2), ("x", "yh", "z", "yl", "core"))
    freq, space = ("x", "yh", "z"), ("yl", "core")
    return jax.shard_map(
        body,
        mesh=fine,
        in_specs=(
            P(None, freq, None, None, None, space),
            P(space),
            P(None, freq, None),
            P(None, freq),
        ),
        out_specs=P(None, freq, None, None),
        check_vma=False,
    )
```

```python
import jax
import jax.numpy as jnp
from jax import lax
from jax.experimental import pallas as pl
from jax.experimental.pallas import tpu as pltpu
from jax.sharding import Mesh
from jax.sharding import PartitionSpec as P

F32, BF16 = jnp.float32, jnp.bfloat16
LANES = 128
MIB = 1024 * 1024


def split_kernel(x_ref, triads_ref, weights_ref, out_ref):
    block = lax.broadcasted_iota(jnp.int32, (24, LANES), 1) // 16
    for q in range(6):
        sources = [x_ref[8 * q + s].astype(F32) for s in range(8)]
        for piece in range(8):
            built = None
            for s in range(8):
                shift = (s - piece) % 8 * 16
                moved = pltpu.roll(sources[s], shift, 1) if shift else sources[s]
                built = moved if built is None else jnp.where(block == s, moved, built)
            out_ref[piece, 24 * q : 24 * q + 24] = built.astype(BF16)
    listed = triads_ref[...]
    rest = weights_ref[...]
    parts = []
    for _ in range(3):
        parts.append(rest.astype(BF16))
        rest = rest - parts[-1].astype(F32)
    for piece in range(8):
        tile = [(listed >> 6).astype(F32), (listed & 63).astype(F32)]
        for part in parts:
            own = part[:, 16 * piece : 16 * piece + 16].astype(F32)
            tile.append(jnp.broadcast_to(own, (8, 16)))
        tile.append(jnp.zeros((8, 48), F32))
        out_ref[piece, 144:152] = jnp.concatenate(tile, axis=1).astype(BF16)


def unpack_kernel(own_ref, sib_ref, *refs):
    bins_ref = refs[-1]
    lane = lax.broadcasted_iota(jnp.int32, (24, LANES), 1)

    @pl.loop(0, 8, unroll=4)
    def _(column):
        tiles = [
            [ref[column, 24 * q : 24 * q + 24].astype(F32) for q in range(6)]
            for ref in (own_ref, sib_ref)
        ]
        for r in range(8):
            for part in range(2):
                q, offset = divmod(96 * r + 48 * part, LANES)
                halves = []
                for core in range(2):
                    picked = tiles[core][q]
                    if offset + 48 > LANES:
                        picked = jnp.where(lane >= offset, picked, tiles[core][q + 1])
                    shift = (48 * core - offset) % LANES
                    halves.append(pltpu.roll(picked, shift, 1) if shift else picked)
                merged = jnp.where(lane < 48, halves[0], halves[1])
                lanes = slice(LANES * part, LANES * (part + 1))
                bins_ref[column * 8 + r, :, lanes] = merged.astype(BF16)


def lane_weights(own_ref, sib_ref):
    lane = lax.broadcasted_iota(jnp.int32, (8, LANES), 1)
    total = jnp.zeros((8, LANES), F32)
    for core, ref in enumerate((own_ref, sib_ref)):
        tile = ref[...].astype(F32)
        for component in range(3):
            begin = 48 * core + 16 * component
            inside = (lane >= begin) & (lane < begin + 16)
            value = sum(pltpu.roll(tile, (begin - 32 - 16 * n) % LANES, 1) for n in range(3))
            total = jnp.where(inside, value, total)
    return total[0:1]


def grams_kernel(triads_ref, own_w_ref, sib_w_ref, bins_ref, out_ref, *scratch):
    buffers = (scratch[0:2], scratch[2:4])
    depth, core = lax.axis_index("z"), lax.axis_index("core")
    up = 1 - 2 * core

    def slot(which):
        turn = (up * (depth - (which & 7))) & 7
        return turn * 64 + (which & 56) + (which >> 6)

    weights = lane_weights(own_w_ref, sib_w_ref)
    lane = lax.broadcasted_iota(jnp.int32, (48, LANES), 1)

    def prepare(reader, buffer):
        w_ref, q_ref = buffer
        owner = reader >> 2
        row = (reader & 2) * 2 + core * 2 + (reader & 1)
        k_bin = row * 64 + owner * 8 + depth
        first = bins_ref[owner * 8 + row].astype(F32)
        k_real = first[:, :LANES] * weights
        k_imag = first[:, LANES:] * weights

        def some(triads):
            for t in triads:
                l_bin = triads_ref[owner * 8 + row, t]
                m_bin = (k_bin + l_bin) & 511
                second = bins_ref[slot(l_bin)].astype(F32)
                l_real, l_imag = second[:, :LANES], second[:, LANES:]
                real = (k_real * l_real - k_imag * l_imag).astype(BF16)
                imag = k_real * l_imag + k_imag * l_real
                plus, minus = imag.astype(BF16), (-imag).astype(BF16)
                w_ref[48 * t : 48 * t + 24, :LANES] = real
                w_ref[48 * t : 48 * t + 24, LANES:] = plus
                w_ref[48 * t + 24 : 48 * t + 48, :LANES] = minus
                w_ref[48 * t + 24 : 48 * t + 48, LANES:] = real
                q_ref[24 * t : 24 * t + 24, :] = bins_ref[slot(m_bin)]

        return some

    def multiply(reader, buffer, n):
        w_ref, q_ref = buffer
        start = 5 * n
        product = lax.dot_general(
            w_ref[48 * start : 48 * (start + 6), :],
            q_ref[LANES * n : LANES * (n + 1), :],
            (((1,), (1,)), ((), ())),
            preferred_element_type=F32,
        )
        built = product[:48]
        for i in range(1, 6):
            begin = 24 * (start + i) - LANES * n
            built = jnp.where(lane >= begin, product[48 * i : 48 * (i + 1)], built)
        lanes = slice(LANES * n, LANES * (n + 1))
        out_ref[reader >> 1, reader & 1, :, lanes] = built.astype(BF16)

    thirds = (range(0, 5), range(5, 10), range(10, 16))
    ready = prepare(0, buffers[0])
    for third in thirds:
        ready(third)

    @pl.loop(0, 16, unroll=8)
    def _(pair):
        for side in range(2):
            reader = 2 * pair + side
            following = prepare((reader + 1) & 31, buffers[1 - side])
            for n, third in enumerate(thirds):
                multiply(reader, buffers[side], n)
                following(third)


def vmem():
    return pl.BlockSpec(memory_space=pltpu.VMEM)


def smem():
    return pl.BlockSpec(memory_space=pltpu.SMEM)


def step(array, axes, by):
    size = lax.axis_size(axes)
    return lax.ppermute(array, axes, [(i, (i + by) % size) for i in range(size)])


def swap(array):
    return step(array, "core", 1)


def ring(array, crossed=False):
    pairs = []
    for z in range(8):
        up, down = (2 * z + 2) % 16, (2 * z - 2) % 16 + 1
        pairs += [(2 * z, down), (2 * z + 1, up)] if crossed else [(2 * z, up), (2 * z + 1, down)]
    return lax.ppermute(array, ("z", "core"), pairs)


def params(mib):
    return pltpu.CompilerParams(vmem_limit_bytes=mib * MIB)


BINS = jax.ShapeDtypeStruct((512, 24, 256), BF16)


def unpack(own, sib, bins, turn):
    operands = [own, sib] + ([] if bins is None else [bins])
    return pl.pallas_call(
        unpack_kernel,
        out_shape=BINS,
        grid=(1,),
        in_specs=[pl.BlockSpec((8, 144, LANES), lambda i: (0, 0, 0))] * 2
        + [pl.BlockSpec(memory_space=pl.ANY)] * (len(operands) - 2),
        out_specs=pl.BlockSpec((64, 24, 256), lambda i: (turn, 0, 0)),
        input_output_aliases={} if bins is None else {2: 0},
        compiler_params=params(8),
        cost_estimate=pl.CostEstimate(flops=1500000000, bytes_accessed=2000000, transcendentals=0),
        name="unpack",
    )(*operands)


def grams(lists, own_tile, sib_tile, bins):
    return pl.pallas_call(
        grams_kernel,
        out_shape=jax.ShapeDtypeStruct((16, 2, 48, 384), BF16),
        in_specs=[smem()] + [vmem()] * 3,
        out_specs=vmem(),
        scratch_shapes=[pltpu.VMEM((768, 256), BF16), pltpu.VMEM((384, 256), BF16)] * 2,
        compiler_params=params(12),
        cost_estimate=pl.CostEstimate(
            flops=12000000000, bytes_accessed=8000000, transcendentals=0
        ),
        name="grams",
    )(lists, own_tile, sib_tile, bins)


def body(modes, point_weights, triads, counts):
    pieces = pl.pallas_call(
        split_kernel,
        out_shape=jax.ShapeDtypeStruct((8, 152, LANES), BF16),
        in_specs=[vmem()] * 3,
        out_specs=vmem(),
        compiler_params=params(56),
        name="split",
    )(modes.reshape(48, 24, LANES), triads[:, 0], point_weights[None])
    received = lax.all_to_all(pieces, ("x", "yh"), 0, 0)
    codes = received[:, 144:, :32].astype(F32)
    lists = (codes[:, :, :16] * 64 + codes[:, :, 16:]).astype(jnp.int32).reshape(64, 16)

    beside = swap(received)
    near, sib = [received[:, :144]], [beside[:, :144]]
    near.append(ring(near[0]))
    sib.append(ring(near[0], crossed=True))
    for _ in range(2):
        near.append(ring(near[-1]))
        sib.append(ring(sib[-1]))
    near.append(ring(near[-1]))
    bins = unpack(near[0], sib[0], None, 0)
    passed = []
    for s in range(1, 4):
        pair = lax.optimization_barrier((sib[s], near[s]))
        passed.append((swap(pair[0]), swap(pair[1])))
    bins = unpack(near[1], sib[1], bins, 1)
    bins = unpack(*passed[0], bins, 7)
    bins = unpack(near[2], sib[2], bins, 2)
    bins = unpack(*passed[1], bins, 6)
    bins = unpack(near[3], sib[3], bins, 3)
    last, bins = lax.optimization_barrier((near[4], bins))
    last_passed = swap(last)
    bins = unpack(*passed[2], bins, 5)
    bins = unpack(last, last_passed, bins, 4)

    partial = grams(lists, received[0, 144:], beside[0, 144:], bins)
    parts = lax.all_to_all(partial, ("x", "yh", "yl"), 0, 0)
    parts, counts = lax.optimization_barrier((parts, counts))
    summed = jnp.sum(parts.astype(F32), axis=0) / 24
    rows = summed.reshape(2, 48, 16, 24).transpose(0, 2, 1, 3).reshape(2, 1, 16, 1152)
    gathered = lax.all_gather(rows, ("yl", "core"), tiled=True)
    live = jnp.arange(16, dtype=jnp.int32)[None, None, :, None] < counts[:, :, None, None]
    return jnp.where(live, gathered, 0.0)


def solution(mesh):
    fine = Mesh(mesh.devices.reshape(4, 2, 8, 2, 2), ("x", "yh", "z", "yl", "core"))
    freq, space = ("x", "yh", "z"), ("yl", "core")
    return jax.shard_map(
        body,
        mesh=fine,
        in_specs=(
            P(None, freq, None, None, None, space),
            P(space),
            P(None, freq, None),
            P(None, freq),
        ),
        out_specs=P(None, freq, None, None),
        check_vma=False,
    )
```

```python
import jax
import jax.numpy as jnp
from jax import lax
from jax.experimental import pallas as pl
from jax.experimental.pallas import tpu as pltpu
from jax.sharding import Mesh
from jax.sharding import PartitionSpec as P

F32, BF16 = jnp.float32, jnp.bfloat16
LANES = 128
MIB = 1024 * 1024


def split_kernel(x_ref, triads_ref, weights_ref, out_ref):
    block = lax.broadcasted_iota(jnp.int32, (24, LANES), 1) // 16
    for q in range(6):
        sources = [x_ref[8 * q + s].astype(F32) for s in range(8)]
        for piece in range(8):
            built = None
            for s in range(8):
                shift = (s - piece) % 8 * 16
                moved = pltpu.roll(sources[s], shift, 1) if shift else sources[s]
                built = moved if built is None else jnp.where(block == s, moved, built)
            out_ref[piece, 24 * q : 24 * q + 24] = built.astype(BF16)
    listed = triads_ref[...]
    rest = weights_ref[...]
    parts = []
    for _ in range(3):
        parts.append(rest.astype(BF16))
        rest = rest - parts[-1].astype(F32)
    for piece in range(8):
        tile = [(listed >> 6).astype(F32), (listed & 63).astype(F32)]
        for part in parts:
            own = part[:, 16 * piece : 16 * piece + 16].astype(F32)
            tile.append(jnp.broadcast_to(own, (8, 16)))
        tile.append(jnp.zeros((8, 48), F32))
        out_ref[piece, 144:152] = jnp.concatenate(tile, axis=1).astype(BF16)


def unpack_kernel(*refs):
    bins_ref = refs[-1]
    lane = lax.broadcasted_iota(jnp.int32, (24, LANES), 1)
    for half in range(2):

        @pl.loop(0, 4, unroll=2)
        def _(column, half=half):
            tiles = [
                [ref[column, 24 * q : 24 * q + 24].astype(F32) for q in range(6)]
                for ref in (refs[half], refs[2 + half])
            ]
            for r in range(8):
                for part in range(2):
                    q, offset = divmod(96 * r + 48 * part, LANES)
                    pair = []
                    for core in range(2):
                        picked = tiles[core][q]
                        if offset + 48 > LANES:
                            picked = jnp.where(lane >= offset, picked, tiles[core][q + 1])
                        shift = (48 * core - offset) % LANES
                        pair.append(pltpu.roll(picked, shift, 1) if shift else picked)
                    merged = jnp.where(lane < 48, pair[0], pair[1])
                    lanes = slice(LANES * part, LANES * (part + 1))
                    bins_ref[(half * 4 + column) * 8 + r, :, lanes] = merged.astype(BF16)


def lane_weights(own_ref, sib_ref):
    lane = lax.broadcasted_iota(jnp.int32, (8, LANES), 1)
    total = jnp.zeros((8, LANES), F32)
    for core, ref in enumerate((own_ref, sib_ref)):
        tile = ref[...].astype(F32)
        for component in range(3):
            begin = 48 * core + 16 * component
            inside = (lane >= begin) & (lane < begin + 16)
            value = sum(pltpu.roll(tile, (begin - 32 - 16 * n) % LANES, 1) for n in range(3))
            total = jnp.where(inside, value, total)
    return total[0:1]


def grams_kernel(triads_ref, own_w_ref, sib_w_ref, bins_ref, out_ref, *scratch):
    buffers = (scratch[0:2], scratch[2:4])
    depth, core = lax.axis_index("z"), lax.axis_index("core")

    def slot(which):
        turn = (depth - (which & 7)) & 7
        return turn * 64 + (which & 56) + (which >> 6)

    weights = lane_weights(own_w_ref, sib_w_ref)
    lane = lax.broadcasted_iota(jnp.int32, (48, LANES), 1)

    def prepare(reader, buffer):
        w_ref, q_ref = buffer
        owner = reader >> 2
        row = (reader & 2) * 2 + core * 2 + (reader & 1)
        k_bin = row * 64 + owner * 8 + depth
        first = bins_ref[owner * 8 + row].astype(F32)
        k_real = first[:, :LANES] * weights
        k_imag = first[:, LANES:] * weights

        def some(triads):
            for t in triads:
                l_bin = triads_ref[owner * 8 + row, t]
                m_bin = (k_bin + l_bin) & 511
                second = bins_ref[slot(l_bin)].astype(F32)
                l_real, l_imag = second[:, :LANES], second[:, LANES:]
                real = (k_real * l_real - k_imag * l_imag).astype(BF16)
                imag = k_real * l_imag + k_imag * l_real
                plus, minus = imag.astype(BF16), (-imag).astype(BF16)
                w_ref[48 * t : 48 * t + 24, :LANES] = real
                w_ref[48 * t : 48 * t + 24, LANES:] = plus
                w_ref[48 * t + 24 : 48 * t + 48, :LANES] = minus
                w_ref[48 * t + 24 : 48 * t + 48, LANES:] = real
                q_ref[24 * t : 24 * t + 24, :] = bins_ref[slot(m_bin)]

        return some

    def multiply(reader, buffer, n):
        w_ref, q_ref = buffer
        start = 5 * n
        product = lax.dot_general(
            w_ref[48 * start : 48 * (start + 6), :],
            q_ref[LANES * n : LANES * (n + 1), :],
            (((1,), (1,)), ((), ())),
            preferred_element_type=F32,
        )
        built = product[:48]
        for i in range(1, 6):
            begin = 24 * (start + i) - LANES * n
            built = jnp.where(lane >= begin, product[48 * i : 48 * (i + 1)], built)
        lanes = slice(LANES * n, LANES * (n + 1))
        out_ref[reader >> 1, reader & 1, :, lanes] = built.astype(BF16)

    thirds = (range(0, 5), range(5, 10), range(10, 16))
    ready = prepare(0, buffers[0])
    for third in thirds:
        ready(third)

    @pl.loop(0, 16, unroll=8)
    def _(pair):
        for side in range(2):
            reader = 2 * pair + side
            following = prepare((reader + 1) & 31, buffers[1 - side])
            for n, third in enumerate(thirds):
                multiply(reader, buffers[side], n)
                following(third)


def vmem():
    return pl.BlockSpec(memory_space=pltpu.VMEM)


def smem():
    return pl.BlockSpec(memory_space=pltpu.SMEM)


def step(array, axes, by):
    size = lax.axis_size(axes)
    return lax.ppermute(array, axes, [(i, (i + by) % size) for i in range(size)])


def swap(array):
    return step(array, "core", 1)


def params(mib):
    return pltpu.CompilerParams(vmem_limit_bytes=mib * MIB)


BINS = jax.ShapeDtypeStruct((512, 24, 256), BF16)


def unpack(parts, bins, turn):
    specs = [pl.BlockSpec((4, 144, LANES), lambda i, at=at: (at, 0, 0)) for _, at in parts]
    operands = [array for array, _ in parts] + ([] if bins is None else [bins])
    return pl.pallas_call(
        unpack_kernel,
        out_shape=BINS,
        grid=(1,),
        in_specs=specs + [pl.BlockSpec(memory_space=pl.ANY)] * (len(operands) - 4),
        out_specs=pl.BlockSpec((64, 24, 256), lambda i: (turn, 0, 0)),
        input_output_aliases={} if bins is None else {4: 0},
        compiler_params=params(8),
        cost_estimate=pl.CostEstimate(flops=1500000000, bytes_accessed=2000000, transcendentals=0),
        name="unpack",
    )(*operands)


def grams(lists, own_tile, sib_tile, bins):
    return pl.pallas_call(
        grams_kernel,
        out_shape=jax.ShapeDtypeStruct((16, 2, 48, 384), BF16),
        in_specs=[smem()] + [vmem()] * 3,
        out_specs=vmem(),
        scratch_shapes=[pltpu.VMEM((768, 256), BF16), pltpu.VMEM((384, 256), BF16)] * 2,
        compiler_params=params(12),
        cost_estimate=pl.CostEstimate(
            flops=12000000000, bytes_accessed=8000000, transcendentals=0
        ),
        name="grams",
    )(lists, own_tile, sib_tile, bins)


def body(modes, point_weights, triads, counts):
    pieces = pl.pallas_call(
        split_kernel,
        out_shape=jax.ShapeDtypeStruct((8, 152, LANES), BF16),
        in_specs=[vmem()] * 3,
        out_specs=vmem(),
        compiler_params=params(56),
        name="split",
    )(modes.reshape(48, 24, LANES), triads[:, 0], point_weights[None])
    received = lax.all_to_all(pieces, ("x", "yh"), 0, 0)
    codes = received[:, 144:, :32].astype(F32)
    lists = (codes[:, :, :16] * 64 + codes[:, :, 16:]).astype(jnp.int32).reshape(64, 16)

    beside = swap(received)
    own, sib = received[:, :144], beside[:, :144]
    up, down = [[own[:4], own[4:]]], [[own[:4], own[4:]]]
    passed = []
    for s in range(3):
        up.append([step(part, "z", 1) for part in up[s]])
        down.append([step(part, "z", -1) for part in down[s]])
        passed.append(swap(jnp.concatenate(up[-1] + down[-1])))
    far = [step(up[3][0], "z", 1), step(down[3][1], "z", -1)]
    bins = unpack([(own, 0), (own, 1), (sib, 0), (sib, 1)], None, 0)
    for s in range(3):
        if s == 2:
            far[0], far[1], bins = lax.optimization_barrier((far[0], far[1], bins))
            last = swap(jnp.concatenate(far))
        mine, theirs = up[s + 1] + down[s + 1], passed[s]
        for way, turn in ((0, s + 1), (2, 7 - s)):
            operands = [(mine[way], 0), (mine[way + 1], 0), (theirs, way), (theirs, way + 1)]
            bins = unpack(operands, bins, turn)
    bins = unpack([(far[0], 0), (far[1], 0), (last, 0), (last, 1)], bins, 4)

    partial = grams(lists, received[0, 144:], beside[0, 144:], bins)
    parts = lax.all_to_all(partial, ("x", "yh", "yl"), 0, 0)
    parts, counts = lax.optimization_barrier((parts, counts))
    summed = jnp.sum(parts.astype(F32), axis=0) / 24
    rows = summed.reshape(2, 48, 16, 24).transpose(0, 2, 1, 3).reshape(2, 1, 16, 1152)
    gathered = lax.all_gather(rows, ("yl", "core"), tiled=True)
    live = jnp.arange(16, dtype=jnp.int32)[None, None, :, None] < counts[:, :, None, None]
    return jnp.where(live, gathered, 0.0)


def solution(mesh):
    fine = Mesh(mesh.devices.reshape(4, 2, 8, 2, 2), ("x", "yh", "z", "yl", "core"))
    freq, space = ("x", "yh", "z"), ("yl", "core")
    return jax.shard_map(
        body,
        mesh=fine,
        in_specs=(
            P(None, freq, None, None, None, space),
            P(space),
            P(None, freq, None),
            P(None, freq),
        ),
        out_specs=P(None, freq, None, None),
        check_vma=False,
    )
```

```python
import jax
import jax.numpy as jnp
from jax import lax
from jax.experimental import pallas as pl
from jax.experimental.pallas import tpu as pltpu
from jax.sharding import Mesh
from jax.sharding import PartitionSpec as P

F32, BF16 = jnp.float32, jnp.bfloat16
LANES = 128
MIB = 1024 * 1024


def split_kernel(x_ref, triads_ref, weights_ref, out_ref):
    block = lax.broadcasted_iota(jnp.int32, (24, LANES), 1) // 16
    for q in range(6):
        sources = [x_ref[8 * q + s].astype(F32) for s in range(8)]
        for piece in range(8):
            built = None
            for s in range(8):
                shift = (s - piece) % 8 * 16
                moved = pltpu.roll(sources[s], shift, 1) if shift else sources[s]
                built = moved if built is None else jnp.where(block == s, moved, built)
            out_ref[piece, 24 * q : 24 * q + 24] = built.astype(BF16)
    listed = triads_ref[...]
    rest = weights_ref[...]
    parts = []
    for _ in range(3):
        parts.append(rest.astype(BF16))
        rest = rest - parts[-1].astype(F32)
    for piece in range(8):
        tile = [(listed >> 6).astype(F32), (listed & 63).astype(F32)]
        for part in parts:
            own = part[:, 16 * piece : 16 * piece + 16].astype(F32)
            tile.append(jnp.broadcast_to(own, (8, 16)))
        tile.append(jnp.zeros((8, 48), F32))
        out_ref[piece, 144:152] = jnp.concatenate(tile, axis=1).astype(BF16)


def unpack_kernel(own_ref, sib_ref, *refs):
    bins_ref = refs[-1]
    lane = lax.broadcasted_iota(jnp.int32, (24, LANES), 1)

    @pl.loop(0, 8, unroll=4)
    def _(column):
        tiles = [
            [ref[column, 24 * q : 24 * q + 24].astype(F32) for q in range(6)]
            for ref in (own_ref, sib_ref)
        ]
        for r in range(8):
            for part in range(2):
                q, offset = divmod(96 * r + 48 * part, LANES)
                halves = []
                for core in range(2):
                    picked = tiles[core][q]
                    if offset + 48 > LANES:
                        picked = jnp.where(lane >= offset, picked, tiles[core][q + 1])
                    shift = (48 * core - offset) % LANES
                    halves.append(pltpu.roll(picked, shift, 1) if shift else picked)
                merged = jnp.where(lane < 48, halves[0], halves[1])
                lanes = slice(LANES * part, LANES * (part + 1))
                bins_ref[column * 8 + r, :, lanes] = merged.astype(BF16)


def lane_weights(own_ref, sib_ref):
    lane = lax.broadcasted_iota(jnp.int32, (8, LANES), 1)
    total = jnp.zeros((8, LANES), F32)
    for core, ref in enumerate((own_ref, sib_ref)):
        tile = ref[...].astype(F32)
        for component in range(3):
            begin = 48 * core + 16 * component
            inside = (lane >= begin) & (lane < begin + 16)
            value = sum(pltpu.roll(tile, (begin - 32 - 16 * n) % LANES, 1) for n in range(3))
            total = jnp.where(inside, value, total)
    return total[0:1]


def grams_kernel(triads_ref, own_w_ref, sib_w_ref, bins_ref, out_ref, *scratch):
    buffers = (scratch[0:2], scratch[2:4])
    depth, core = lax.axis_index("z"), lax.axis_index("core")
    up = 1 - 2 * core

    def slot(which):
        turn = (up * (depth - (which & 7))) & 7
        return turn * 64 + (which & 8) * 4 + (which & 48) // 2 + (which >> 6)

    weights = lane_weights(own_w_ref, sib_w_ref)
    lane = lax.broadcasted_iota(jnp.int32, (48, LANES), 1)

    def prepare(reader, buffer):
        w_ref, q_ref = buffer
        owner = reader >> 2
        row = (reader & 2) * 2 + core * 2 + (reader & 1)
        k_bin = row * 64 + (owner & 3) * 16 + (owner >> 2) * 8 + depth
        first = bins_ref[owner * 8 + row].astype(F32)
        k_real = first[:, :LANES] * weights
        k_imag = first[:, LANES:] * weights

        def some(triads):
            for t in triads:
                l_bin = triads_ref[owner * 8 + row, t]
                m_bin = (k_bin + l_bin) & 511
                second = bins_ref[slot(l_bin)].astype(F32)
                l_real, l_imag = second[:, :LANES], second[:, LANES:]
                real = (k_real * l_real - k_imag * l_imag).astype(BF16)
                imag = k_real * l_imag + k_imag * l_real
                plus, minus = imag.astype(BF16), (-imag).astype(BF16)
                w_ref[48 * t : 48 * t + 24, :LANES] = real
                w_ref[48 * t : 48 * t + 24, LANES:] = plus
                w_ref[48 * t + 24 : 48 * t + 48, :LANES] = minus
                w_ref[48 * t + 24 : 48 * t + 48, LANES:] = real
                q_ref[24 * t : 24 * t + 24, :] = bins_ref[slot(m_bin)]

        return some

    def multiply(reader, buffer, n):
        w_ref, q_ref = buffer
        start = 5 * n
        product = lax.dot_general(
            w_ref[48 * start : 48 * (start + 6), :],
            q_ref[LANES * n : LANES * (n + 1), :],
            (((1,), (1,)), ((), ())),
            preferred_element_type=F32,
        )
        built = product[:48]
        for i in range(1, 6):
            begin = 24 * (start + i) - LANES * n
            built = jnp.where(lane >= begin, product[48 * i : 48 * (i + 1)], built)
        lanes = slice(LANES * n, LANES * (n + 1))
        place = ((reader >> 2) & 3) * 4 + (reader & 2) + (reader >> 4)
        out_ref[place, reader & 1, :, lanes] = built.astype(BF16)

    thirds = (range(0, 5), range(5, 10), range(10, 16))
    ready = prepare(0, buffers[0])
    for third in thirds:
        ready(third)

    @pl.loop(0, 16, unroll=8)
    def _(pair):
        for side in range(2):
            reader = 2 * pair + side
            following = prepare((reader + 1) & 31, buffers[1 - side])
            for n, third in enumerate(thirds):
                multiply(reader, buffers[side], n)
                following(third)


def vmem():
    return pl.BlockSpec(memory_space=pltpu.VMEM)


def smem():
    return pl.BlockSpec(memory_space=pltpu.SMEM)


def step(array, axes, by):
    size = lax.axis_size(axes)
    return lax.ppermute(array, axes, [(i, (i + by) % size) for i in range(size)])


def swap(array):
    return step(array, "core", 1)


def ring(array, crossed=False):
    pairs = []
    for z in range(8):
        up, down = (2 * z + 2) % 16, (2 * z - 2) % 16 + 1
        pairs += [(2 * z, down), (2 * z + 1, up)] if crossed else [(2 * z, up), (2 * z + 1, down)]
    return lax.ppermute(array, ("z", "core"), pairs)


def params(mib):
    return pltpu.CompilerParams(vmem_limit_bytes=mib * MIB)


BINS = jax.ShapeDtypeStruct((512, 24, 256), BF16)


def unpack(own, sib, bins, turn):
    operands = [own, sib] + ([] if bins is None else [bins])
    return pl.pallas_call(
        unpack_kernel,
        out_shape=BINS,
        grid=(1,),
        in_specs=[pl.BlockSpec((8, 144, LANES), lambda i: (0, 0, 0))] * 2
        + [pl.BlockSpec(memory_space=pl.ANY)] * (len(operands) - 2),
        out_specs=pl.BlockSpec((64, 24, 256), lambda i: (turn, 0, 0)),
        input_output_aliases={} if bins is None else {2: 0},
        compiler_params=params(8),
        cost_estimate=pl.CostEstimate(flops=1500000000, bytes_accessed=2000000, transcendentals=0),
        name="unpack",
    )(*operands)


def grams(lists, own_tile, sib_tile, bins):
    return pl.pallas_call(
        grams_kernel,
        out_shape=jax.ShapeDtypeStruct((16, 2, 48, 384), BF16),
        in_specs=[smem()] + [vmem()] * 3,
        out_specs=vmem(),
        scratch_shapes=[pltpu.VMEM((768, 256), BF16), pltpu.VMEM((384, 256), BF16)] * 2,
        compiler_params=params(12),
        cost_estimate=pl.CostEstimate(
            flops=12000000000, bytes_accessed=8000000, transcendentals=0
        ),
        name="grams",
    )(lists, own_tile, sib_tile, bins)


def body(modes, point_weights, triads, counts):
    pieces = pl.pallas_call(
        split_kernel,
        out_shape=jax.ShapeDtypeStruct((8, 152, LANES), BF16),
        in_specs=[vmem()] * 3,
        out_specs=vmem(),
        compiler_params=params(56),
        name="split",
    )(modes.reshape(48, 24, LANES), triads[:, 0], point_weights[None])
    received = lax.all_to_all(pieces, ("yh", "x"), 0, 0)
    codes = received[:, 144:, :32].astype(F32)
    lists = (codes[:, :, :16] * 64 + codes[:, :, 16:]).astype(jnp.int32).reshape(64, 16)

    beside = swap(received)
    near, sib = [received[:, :144]], [beside[:, :144]]
    near.append(ring(near[0]))
    sib.append(ring(near[0], crossed=True))
    for _ in range(2):
        near.append(ring(near[-1]))
        sib.append(ring(sib[-1]))
    near.append(ring(near[-1]))
    bins = unpack(near[0], sib[0], None, 0)
    passed = []
    for s in range(1, 4):
        pair = lax.optimization_barrier((sib[s], near[s]))
        passed.append((swap(pair[0]), swap(pair[1])))
    bins = unpack(near[1], sib[1], bins, 1)
    bins = unpack(*passed[0], bins, 7)
    bins = unpack(near[2], sib[2], bins, 2)
    bins = unpack(*passed[1], bins, 6)
    bins = unpack(near[3], sib[3], bins, 3)
    last, bins = lax.optimization_barrier((near[4], bins))
    last_passed = swap(last)
    bins = unpack(*passed[2], bins, 5)
    bins = unpack(last, last_passed, bins, 4)

    partial = grams(lists, received[0, 144:], beside[0, 144:], bins)
    parts = lax.all_to_all(partial, ("x", "yl", "yh"), 0, 0)
    parts, counts = lax.optimization_barrier((parts, counts))
    summed = jnp.sum(parts.astype(F32), axis=0) / 24
    rows = summed.reshape(2, 48, 16, 24).transpose(0, 2, 1, 3).reshape(2, 1, 16, 1152)
    gathered = lax.all_gather(rows, ("yl", "core"), tiled=True)
    live = jnp.arange(16, dtype=jnp.int32)[None, None, :, None] < counts[:, :, None, None]
    return jnp.where(live, gathered, 0.0)


def solution(mesh):
    fine = Mesh(mesh.devices.reshape(4, 2, 8, 2, 2), ("x", "yh", "z", "yl", "core"))
    freq, space = ("x", "yh", "z"), ("yl", "core")
    return jax.shard_map(
        body,
        mesh=fine,
        in_specs=(
            P(None, freq, None, None, None, space),
            P(space),
            P(None, freq, None),
            P(None, freq),
        ),
        out_specs=P(None, freq, None, None),
        check_vma=False,
    )
```

```python
import jax
import jax.numpy as jnp
from jax import lax
from jax.experimental import pallas as pl
from jax.experimental.pallas import tpu as pltpu
from jax.sharding import Mesh
from jax.sharding import PartitionSpec as P

F32, BF16 = jnp.float32, jnp.bfloat16
LANES = 128
MIB = 1024 * 1024


def split_kernel(x_ref, triads_ref, weights_ref, out_ref):
    block = lax.broadcasted_iota(jnp.int32, (24, LANES), 1) // 16
    for q in range(6):
        sources = [x_ref[8 * q + s].astype(F32) for s in range(8)]
        for piece in range(8):
            built = None
            for s in range(8):
                shift = (s - piece) % 8 * 16
                moved = pltpu.roll(sources[s], shift, 1) if shift else sources[s]
                built = moved if built is None else jnp.where(block == s, moved, built)
            out_ref[piece, 24 * q : 24 * q + 24] = built.astype(BF16)
    listed = triads_ref[...]
    rest = weights_ref[...]
    parts = []
    for _ in range(3):
        parts.append(rest.astype(BF16))
        rest = rest - parts[-1].astype(F32)
    for piece in range(8):
        tile = [(listed >> 6).astype(F32), (listed & 63).astype(F32)]
        for part in parts:
            own = part[:, 16 * piece : 16 * piece + 16].astype(F32)
            tile.append(jnp.broadcast_to(own, (8, 16)))
        tile.append(jnp.zeros((8, 48), F32))
        out_ref[piece, 144:152] = jnp.concatenate(tile, axis=1).astype(BF16)


def unpack_kernel(own_ref, sib_ref, *refs):
    bins_ref = refs[-1]
    lane = lax.broadcasted_iota(jnp.int32, (24, LANES), 1)

    @pl.loop(0, 8, unroll=4)
    def _(column):
        tiles = [
            [ref[column, 24 * q : 24 * q + 24].astype(F32) for q in range(6)]
            for ref in (own_ref, sib_ref)
        ]
        for r in range(8):
            for part in range(2):
                q, offset = divmod(96 * r + 48 * part, LANES)
                halves = []
                for core in range(2):
                    picked = tiles[core][q]
                    if offset + 48 > LANES:
                        picked = jnp.where(lane >= offset, picked, tiles[core][q + 1])
                    shift = (48 * core - offset) % LANES
                    halves.append(pltpu.roll(picked, shift, 1) if shift else picked)
                merged = jnp.where(lane < 48, halves[0], halves[1])
                lanes = slice(LANES * part, LANES * (part + 1))
                bins_ref[column * 8 + r, :, lanes] = merged.astype(BF16)


def lane_weights(own_ref, sib_ref):
    lane = lax.broadcasted_iota(jnp.int32, (8, LANES), 1)
    total = jnp.zeros((8, LANES), F32)
    for core, ref in enumerate((own_ref, sib_ref)):
        tile = ref[...].astype(F32)
        for component in range(3):
            begin = 48 * core + 16 * component
            inside = (lane >= begin) & (lane < begin + 16)
            value = sum(pltpu.roll(tile, (begin - 32 - 16 * n) % LANES, 1) for n in range(3))
            total = jnp.where(inside, value, total)
    return total[0:1]


def grams_kernel(slots_ref, own_w_ref, sib_w_ref, bins_ref, out_ref, *scratch):
    buffers = (scratch[0:2], scratch[2:4])
    core = lax.axis_index("core")
    weights = lane_weights(own_w_ref, sib_w_ref)
    lane = lax.broadcasted_iota(jnp.int32, (48, LANES), 1)

    def prepare(reader, buffer):
        w_ref, q_ref = buffer
        owner = reader >> 2
        row = (reader & 2) * 2 + core * 2 + (reader & 1)
        listed = owner * 8 + row
        first = bins_ref[listed].astype(F32)
        k_real = first[:, :LANES] * weights
        k_imag = first[:, LANES:] * weights

        def some(triads):
            for t in triads:
                second = bins_ref[slots_ref[listed, t]].astype(F32)
                l_real, l_imag = second[:, :LANES], second[:, LANES:]
                real = (k_real * l_real - k_imag * l_imag).astype(BF16)
                imag = k_real * l_imag + k_imag * l_real
                plus, minus = imag.astype(BF16), (-imag).astype(BF16)
                w_ref[48 * t : 48 * t + 24, :LANES] = real
                w_ref[48 * t : 48 * t + 24, LANES:] = plus
                w_ref[48 * t + 24 : 48 * t + 48, :LANES] = minus
                w_ref[48 * t + 24 : 48 * t + 48, LANES:] = real
                q_ref[24 * t : 24 * t + 24, :] = bins_ref[slots_ref[listed, 16 + t]]

        return some

    def multiply(reader, buffer, n):
        w_ref, q_ref = buffer
        start = 5 * n
        product = lax.dot_general(
            w_ref[48 * start : 48 * (start + 6), :],
            q_ref[LANES * n : LANES * (n + 1), :],
            (((1,), (1,)), ((), ())),
            preferred_element_type=F32,
        )
        built = product[:48]
        for i in range(1, 6):
            begin = 24 * (start + i) - LANES * n
            built = jnp.where(lane >= begin, product[48 * i : 48 * (i + 1)], built)
        lanes = slice(LANES * n, LANES * (n + 1))
        out_ref[reader >> 1, reader & 1, :, lanes] = built.astype(BF16)

    thirds = (range(0, 5), range(5, 10), range(10, 16))
    ready = prepare(0, buffers[0])
    for third in thirds:
        ready(third)

    @pl.loop(0, 16, unroll=8)
    def _(pair):
        for side in range(2):
            reader = 2 * pair + side
            following = prepare((reader + 1) & 31, buffers[1 - side])
            for n, third in enumerate(thirds):
                multiply(reader, buffers[side], n)
                following(third)


def vmem():
    return pl.BlockSpec(memory_space=pltpu.VMEM)


def smem():
    return pl.BlockSpec(memory_space=pltpu.SMEM)


def step(array, axes, by):
    size = lax.axis_size(axes)
    return lax.ppermute(array, axes, [(i, (i + by) % size) for i in range(size)])


def swap(array):
    return step(array, "core", 1)


def ring(array, crossed=False):
    pairs = []
    for z in range(8):
        up, down = (2 * z + 2) % 16, (2 * z - 2) % 16 + 1
        pairs += [(2 * z, down), (2 * z + 1, up)] if crossed else [(2 * z, up), (2 * z + 1, down)]
    return lax.ppermute(array, ("z", "core"), pairs)


def params(mib):
    return pltpu.CompilerParams(vmem_limit_bytes=mib * MIB)


BINS = jax.ShapeDtypeStruct((512, 24, 256), BF16)


def unpack(own, sib, bins, turn):
    operands = [own, sib] + ([] if bins is None else [bins])
    return pl.pallas_call(
        unpack_kernel,
        out_shape=BINS,
        grid=(1,),
        in_specs=[pl.BlockSpec((8, 144, LANES), lambda i: (0, 0, 0))] * 2
        + [pl.BlockSpec(memory_space=pl.ANY)] * (len(operands) - 2),
        out_specs=pl.BlockSpec((64, 24, 256), lambda i: (turn, 0, 0)),
        input_output_aliases={} if bins is None else {2: 0},
        compiler_params=params(8),
        cost_estimate=pl.CostEstimate(flops=1500000000, bytes_accessed=2000000, transcendentals=0),
        name="unpack",
    )(*operands)


def grams(slots, own_tile, sib_tile, bins):
    return pl.pallas_call(
        grams_kernel,
        out_shape=jax.ShapeDtypeStruct((16, 2, 48, 384), BF16),
        in_specs=[smem()] + [vmem()] * 3,
        out_specs=vmem(),
        scratch_shapes=[pltpu.VMEM((768, 256), BF16), pltpu.VMEM((384, 256), BF16)] * 2,
        compiler_params=params(12),
        cost_estimate=pl.CostEstimate(
            flops=12000000000, bytes_accessed=8000000, transcendentals=0
        ),
        name="grams",
    )(slots, own_tile, sib_tile, bins)


def body(modes, point_weights, triads, counts):
    pieces = pl.pallas_call(
        split_kernel,
        out_shape=jax.ShapeDtypeStruct((8, 152, LANES), BF16),
        in_specs=[vmem()] * 3,
        out_specs=vmem(),
        compiler_params=params(56),
        name="split",
    )(modes.reshape(48, 24, LANES), triads[:, 0], point_weights[None])
    received = lax.all_to_all(pieces, ("x", "yh"), 0, 0)
    codes = received[:, 144:, :32].astype(F32)
    seconds = (codes[:, :, :16] * 64 + codes[:, :, 16:]).astype(jnp.int32)
    depth, core = lax.axis_index("z"), lax.axis_index("core")
    shape = (8, 8, 1)
    firsts = lax.broadcasted_iota(jnp.int32, shape, 1) * 64
    firsts = firsts + lax.broadcasted_iota(jnp.int32, shape, 0) * 8 + depth
    both = jnp.concatenate([seconds, (firsts + seconds) & 511], axis=2)
    turn = ((1 - 2 * core) * (depth - (both & 7))) & 7
    slots = (turn * 64 + (both & 56) + (both >> 6)).reshape(64, 32)

    beside = swap(received)
    near, sib = [received[:, :144]], [beside[:, :144]]
    near.append(ring(near[0]))
    sib.append(ring(near[0], crossed=True))
    for _ in range(2):
        near.append(ring(near[-1]))
        sib.append(ring(sib[-1]))
    near.append(ring(near[-1]))
    bins = unpack(near[0], sib[0], None, 0)
    passed = []
    for s in range(1, 4):
        pair = lax.optimization_barrier((sib[s], near[s]))
        passed.append((swap(pair[0]), swap(pair[1])))
    bins = unpack(near[1], sib[1], bins, 1)
    bins = unpack(*passed[0], bins, 7)
    bins = unpack(near[2], sib[2], bins, 2)
    bins = unpack(*passed[1], bins, 6)
    bins = unpack(near[3], sib[3], bins, 3)
    last, bins = lax.optimization_barrier((near[4], bins))
    last_passed = swap(last)
    bins = unpack(*passed[2], bins, 5)
    bins = unpack(last, last_passed, bins, 4)

    partial = grams(slots, received[0, 144:], beside[0, 144:], bins)
    parts = lax.all_to_all(partial, ("x", "yh", "yl"), 0, 0)
    parts, counts = lax.optimization_barrier((parts, counts))
    summed = jnp.sum(parts.astype(F32), axis=0) / 24
    rows = summed.reshape(2, 48, 16, 24).transpose(0, 2, 1, 3).reshape(2, 1, 16, 1152)
    gathered = lax.all_gather(rows, ("yl", "core"), tiled=True)
    live = jnp.arange(16, dtype=jnp.int32)[None, None, :, None] < counts[:, :, None, None]
    return jnp.where(live, gathered, 0.0)


def solution(mesh):
    fine = Mesh(mesh.devices.reshape(4, 2, 8, 2, 2), ("x", "yh", "z", "yl", "core"))
    freq, space = ("x", "yh", "z"), ("yl", "core")
    return jax.shard_map(
        body,
        mesh=fine,
        in_specs=(
            P(None, freq, None, None, None, space),
            P(space),
            P(None, freq, None),
            P(None, freq),
        ),
        out_specs=P(None, freq, None, None),
        check_vma=False,
    )
```

```python
import jax
import jax.numpy as jnp
from jax import lax
from jax.experimental import pallas as pl
from jax.experimental.pallas import tpu as pltpu
from jax.sharding import Mesh
from jax.sharding import PartitionSpec as P

F32, BF16 = jnp.float32, jnp.bfloat16
LANES = 128
MIB = 1024 * 1024


def split_kernel(x_ref, triads_ref, weights_ref, out_ref):
    block = lax.broadcasted_iota(jnp.int32, (24, LANES), 1) // 16
    for q in range(6):
        sources = [x_ref[8 * q + s].astype(F32) for s in range(8)]
        for piece in range(8):
            built = None
            for s in range(8):
                shift = (s - piece) % 8 * 16
                moved = pltpu.roll(sources[s], shift, 1) if shift else sources[s]
                built = moved if built is None else jnp.where(block == s, moved, built)
            out_ref[piece, 24 * q : 24 * q + 24] = built.astype(BF16)
    listed = triads_ref[...]
    rest = weights_ref[...]
    parts = []
    for _ in range(3):
        parts.append(rest.astype(BF16))
        rest = rest - parts[-1].astype(F32)
    for piece in range(8):
        tile = [(listed >> 6).astype(F32), (listed & 63).astype(F32)]
        for part in parts:
            own = part[:, 16 * piece : 16 * piece + 16].astype(F32)
            tile.append(jnp.broadcast_to(own, (8, 16)))
        tile.append(jnp.zeros((8, 48), F32))
        out_ref[piece, 144:152] = jnp.concatenate(tile, axis=1).astype(BF16)


def unpack_kernel(own_ref, sib_ref, *refs):
    bins_ref = refs[-1]
    lane = lax.broadcasted_iota(jnp.int32, (24, LANES), 1)

    @pl.loop(0, 8, unroll=4)
    def _(column):
        tiles = [
            [ref[column, 24 * q : 24 * q + 24].astype(F32) for q in range(6)]
            for ref in (own_ref, sib_ref)
        ]
        for r in range(8):
            for part in range(2):
                q, offset = divmod(96 * r + 48 * part, LANES)
                halves = []
                for core in range(2):
                    picked = tiles[core][q]
                    if offset + 48 > LANES:
                        picked = jnp.where(lane >= offset, picked, tiles[core][q + 1])
                    shift = (48 * core - offset) % LANES
                    halves.append(pltpu.roll(picked, shift, 1) if shift else picked)
                merged = jnp.where(lane < 48, halves[0], halves[1])
                lanes = slice(LANES * part, LANES * (part + 1))
                bins_ref[column * 8 + r, :, lanes] = merged.astype(BF16)


def lane_weights(own_ref, sib_ref):
    lane = lax.broadcasted_iota(jnp.int32, (8, LANES), 1)
    total = jnp.zeros((8, LANES), F32)
    for core, ref in enumerate((own_ref, sib_ref)):
        tile = ref[...].astype(F32)
        for component in range(3):
            begin = 48 * core + 16 * component
            inside = (lane >= begin) & (lane < begin + 16)
            value = sum(pltpu.roll(tile, (begin - 32 - 16 * n) % LANES, 1) for n in range(3))
            total = jnp.where(inside, value, total)
    return total[0:1]


def grams_kernel(slots_ref, own_w_ref, sib_w_ref, bins_ref, out_ref, *scratch):
    buffers = (scratch[0:2], scratch[2:4])
    core = lax.axis_index("core")
    weights = lane_weights(own_w_ref, sib_w_ref)
    lane = lax.broadcasted_iota(jnp.int32, (48, LANES), 1)

    def prepare(reader, buffer):
        w_ref, q_ref = buffer
        owner = reader >> 2
        row = (reader & 2) * 2 + core * 2 + (reader & 1)
        listed = owner * 8 + row
        first = bins_ref[listed].astype(F32)
        k_real = first[:, :LANES] * weights
        k_imag = first[:, LANES:] * weights

        def some(triads):
            for t in triads:
                second = bins_ref[slots_ref[listed, t]].astype(F32)
                l_real, l_imag = second[:, :LANES], second[:, LANES:]
                real = (k_real * l_real - k_imag * l_imag).astype(BF16)
                imag = k_real * l_imag + k_imag * l_real
                plus, minus = imag.astype(BF16), (-imag).astype(BF16)
                w_ref[48 * t : 48 * t + 24, :LANES] = real
                w_ref[48 * t : 48 * t + 24, LANES:] = plus
                w_ref[48 * t + 24 : 48 * t + 48, :LANES] = minus
                w_ref[48 * t + 24 : 48 * t + 48, LANES:] = real
                q_ref[24 * t : 24 * t + 24, :] = bins_ref[slots_ref[listed, 16 + t]]

        return some

    def multiply(reader, buffer, n):
        w_ref, q_ref = buffer
        start = 5 * n
        product = lax.dot_general(
            w_ref[48 * start : 48 * (start + 6), :],
            q_ref[LANES * n : LANES * (n + 1), :],
            (((1,), (1,)), ((), ())),
            preferred_element_type=F32,
        )
        built = product[:48]
        for i in range(1, 6):
            begin = 24 * (start + i) - LANES * n
            built = jnp.where(lane >= begin, product[48 * i : 48 * (i + 1)], built)
        lanes = slice(LANES * n, LANES * (n + 1))
        out_ref[reader >> 1, reader & 1, :, lanes] = built.astype(BF16)

    thirds = (range(0, 5), range(5, 10), range(10, 16))
    ready = prepare(0, buffers[0])
    for third in thirds:
        ready(third)

    @pl.loop(0, 16, unroll=8)
    def _(pair):
        for side in range(2):
            reader = 2 * pair + side
            following = prepare((reader + 1) & 31, buffers[1 - side])
            for n, third in enumerate(thirds):
                multiply(reader, buffers[side], n)
                following(third)


def vmem():
    return pl.BlockSpec(memory_space=pltpu.VMEM)


def smem():
    return pl.BlockSpec(memory_space=pltpu.SMEM)


def step(array, axes, by):
    size = lax.axis_size(axes)
    return lax.ppermute(array, axes, [(i, (i + by) % size) for i in range(size)])


def swap(array):
    return step(array, "core", 1)


def ring(array, crossed=False):
    pairs = []
    for z in range(8):
        up, down = (2 * z + 2) % 16, (2 * z - 2) % 16 + 1
        pairs += [(2 * z, down), (2 * z + 1, up)] if crossed else [(2 * z, up), (2 * z + 1, down)]
    return lax.ppermute(array, ("z", "core"), pairs)


def params(mib):
    return pltpu.CompilerParams(vmem_limit_bytes=mib * MIB)


BINS = jax.ShapeDtypeStruct((512, 24, 256), BF16)


def unpack(own, sib, bins, turn):
    operands = [own, sib] + ([] if bins is None else [bins])
    return pl.pallas_call(
        unpack_kernel,
        out_shape=BINS,
        grid=(1,),
        in_specs=[pl.BlockSpec((8, 144, LANES), lambda i: (0, 0, 0))] * 2
        + [pl.BlockSpec(memory_space=pl.ANY)] * (len(operands) - 2),
        out_specs=pl.BlockSpec((64, 24, 256), lambda i: (turn, 0, 0)),
        input_output_aliases={} if bins is None else {2: 0},
        compiler_params=params(8),
        cost_estimate=pl.CostEstimate(flops=1000000000, bytes_accessed=2000000, transcendentals=0),
        name="unpack",
    )(*operands)


def grams(slots, own_tile, sib_tile, bins):
    return pl.pallas_call(
        grams_kernel,
        out_shape=jax.ShapeDtypeStruct((16, 2, 48, 384), BF16),
        in_specs=[smem()] + [vmem()] * 3,
        out_specs=vmem(),
        scratch_shapes=[pltpu.VMEM((768, 256), BF16), pltpu.VMEM((384, 256), BF16)] * 2,
        compiler_params=params(12),
        cost_estimate=pl.CostEstimate(
            flops=12000000000, bytes_accessed=8000000, transcendentals=0
        ),
        name="grams",
    )(slots, own_tile, sib_tile, bins)


def body(modes, point_weights, triads, counts):
    pieces = pl.pallas_call(
        split_kernel,
        out_shape=jax.ShapeDtypeStruct((8, 152, LANES), BF16),
        in_specs=[vmem()] * 3,
        out_specs=vmem(),
        compiler_params=params(56),
        name="split",
    )(modes.reshape(48, 24, LANES), triads[:, 0], point_weights[None])
    received = lax.all_to_all(pieces, ("x", "yh"), 0, 0)
    codes = received[:, 144:, :32].astype(F32)
    seconds = (codes[:, :, :16] * 64 + codes[:, :, 16:]).astype(jnp.int32)
    depth, core = lax.axis_index("z"), lax.axis_index("core")
    shape = (8, 8, 1)
    firsts = lax.broadcasted_iota(jnp.int32, shape, 1) * 64
    firsts = firsts + lax.broadcasted_iota(jnp.int32, shape, 0) * 8 + depth
    both = jnp.concatenate([seconds, (firsts + seconds) & 511], axis=2)
    turn = ((1 - 2 * core) * (depth - (both & 7))) & 7
    slots = (turn * 64 + (both & 56) + (both >> 6)).reshape(64, 32)

    beside = swap(received)
    near, sib = [received[:, :144]], [beside[:, :144]]
    near.append(ring(near[0]))
    sib.append(ring(near[0], crossed=True))
    for _ in range(2):
        near.append(ring(near[-1]))
        sib.append(ring(sib[-1]))
    near.append(ring(near[-1]))
    bins = unpack(near[0], sib[0], None, 0)
    passed = []
    for s in range(1, 4):
        pair = lax.optimization_barrier((sib[s], near[s]))
        passed.append((swap(pair[0]), swap(pair[1])))
    bins = unpack(near[1], sib[1], bins, 1)
    bins = unpack(*passed[0], bins, 7)
    bins = unpack(near[2], sib[2], bins, 2)
    bins = unpack(*passed[1], bins, 6)
    bins = unpack(near[3], sib[3], bins, 3)
    last, bins = lax.optimization_barrier((near[4], bins))
    last_passed = swap(last)
    bins = unpack(*passed[2], bins, 5)
    bins = unpack(last, last_passed, bins, 4)

    partial = grams(slots, received[0, 144:], beside[0, 144:], bins)
    parts = lax.all_to_all(partial, ("x", "yh", "yl"), 0, 0)
    parts, counts = lax.optimization_barrier((parts, counts))
    summed = jnp.sum(parts.astype(F32), axis=0) / 24
    rows = summed.reshape(2, 48, 16, 24).transpose(0, 2, 1, 3).reshape(2, 1, 16, 1152)
    gathered = lax.all_gather(rows, ("yl", "core"), tiled=True)
    live = jnp.arange(16, dtype=jnp.int32)[None, None, :, None] < counts[:, :, None, None]
    return jnp.where(live, gathered, 0.0)


def solution(mesh):
    fine = Mesh(mesh.devices.reshape(4, 2, 8, 2, 2), ("x", "yh", "z", "yl", "core"))
    freq, space = ("x", "yh", "z"), ("yl", "core")
    return jax.shard_map(
        body,
        mesh=fine,
        in_specs=(
            P(None, freq, None, None, None, space),
            P(space),
            P(None, freq, None),
            P(None, freq),
        ),
        out_specs=P(None, freq, None, None),
        check_vma=False,
    )
```

```python
import jax
import jax.numpy as jnp
from jax import lax
from jax.experimental import pallas as pl
from jax.experimental.pallas import tpu as pltpu
from jax.sharding import Mesh
from jax.sharding import PartitionSpec as P

F32, BF16 = jnp.float32, jnp.bfloat16
LANES = 128
MIB = 1024 * 1024


def split_kernel(x_ref, triads_ref, weights_ref, out_ref):
    block = lax.broadcasted_iota(jnp.int32, (24, LANES), 1) // 16
    for q in range(6):
        sources = [x_ref[8 * q + s].astype(F32) for s in range(8)]
        for bit in (1, 2, 4):
            high = (block & bit) > 0
            for s in range(8):
                if not s & bit:
                    low_part, high_part = sources[s], sources[s | bit]
                    raised = pltpu.roll(high_part, 16 * bit, 1)
                    lowered = pltpu.roll(low_part, LANES - 16 * bit, 1)
                    sources[s] = jnp.where(high, raised, low_part)
                    sources[s | bit] = jnp.where(high, high_part, lowered)
        for piece in range(8):
            out_ref[piece, 24 * q : 24 * q + 24] = sources[piece].astype(BF16)
    listed = triads_ref[...]
    rest = weights_ref[...]
    parts = []
    for _ in range(3):
        parts.append(rest.astype(BF16))
        rest = rest - parts[-1].astype(F32)
    for piece in range(8):
        tile = [(listed >> 6).astype(F32), (listed & 63).astype(F32)]
        for part in parts:
            own = part[:, 16 * piece : 16 * piece + 16].astype(F32)
            tile.append(jnp.broadcast_to(own, (8, 16)))
        tile.append(jnp.zeros((8, 48), F32))
        out_ref[piece, 144:152] = jnp.concatenate(tile, axis=1).astype(BF16)


def unpack_kernel(own_ref, sib_ref, *refs):
    bins_ref = refs[-1]
    lane = lax.broadcasted_iota(jnp.int32, (24, LANES), 1)

    @pl.loop(0, 8, unroll=4)
    def _(column):
        tiles = [
            [ref[column, 24 * q : 24 * q + 24].astype(F32) for q in range(6)]
            for ref in (own_ref, sib_ref)
        ]
        for r in range(8):
            for part in range(2):
                q, offset = divmod(96 * r + 48 * part, LANES)
                halves = []
                for core in range(2):
                    picked = tiles[core][q]
                    if offset + 48 > LANES:
                        picked = jnp.where(lane >= offset, picked, tiles[core][q + 1])
                    shift = (48 * core - offset) % LANES
                    halves.append(pltpu.roll(picked, shift, 1) if shift else picked)
                merged = jnp.where(lane < 48, halves[0], halves[1])
                lanes = slice(LANES * part, LANES * (part + 1))
                bins_ref[column * 8 + r, :, lanes] = merged.astype(BF16)


def lane_weights(own_ref, sib_ref):
    lane = lax.broadcasted_iota(jnp.int32, (8, LANES), 1)
    total = jnp.zeros((8, LANES), F32)
    for core, ref in enumerate((own_ref, sib_ref)):
        tile = ref[...].astype(F32)
        for component in range(3):
            begin = 48 * core + 16 * component
            inside = (lane >= begin) & (lane < begin + 16)
            value = sum(pltpu.roll(tile, (begin - 32 - 16 * n) % LANES, 1) for n in range(3))
            total = jnp.where(inside, value, total)
    return total[0:1]


def grams_kernel(slots_ref, own_w_ref, sib_w_ref, bins_ref, out_ref, *scratch):
    buffers = (scratch[0:2], scratch[2:4])
    core = lax.axis_index("core")
    weights = lane_weights(own_w_ref, sib_w_ref)
    lane = lax.broadcasted_iota(jnp.int32, (48, LANES), 1)

    def prepare(reader, buffer):
        w_ref, q_ref = buffer
        owner = reader >> 2
        row = (reader & 2) * 2 + core * 2 + (reader & 1)
        listed = owner * 8 + row
        first = bins_ref[listed].astype(F32)
        k_real = first[:, :LANES] * weights
        k_imag = first[:, LANES:] * weights

        def some(triads):
            for t in triads:
                second = bins_ref[slots_ref[listed, t]].astype(F32)
                l_real, l_imag = second[:, :LANES], second[:, LANES:]
                real = (k_real * l_real - k_imag * l_imag).astype(BF16)
                imag = k_real * l_imag + k_imag * l_real
                plus, minus = imag.astype(BF16), (-imag).astype(BF16)
                w_ref[48 * t : 48 * t + 24, :LANES] = real
                w_ref[48 * t : 48 * t + 24, LANES:] = plus
                w_ref[48 * t + 24 : 48 * t + 48, :LANES] = minus
                w_ref[48 * t + 24 : 48 * t + 48, LANES:] = real
                q_ref[24 * t : 24 * t + 24, :] = bins_ref[slots_ref[listed, 16 + t]]

        return some

    def multiply(reader, buffer, n):
        w_ref, q_ref = buffer
        start = 5 * n
        product = lax.dot_general(
            w_ref[48 * start : 48 * (start + 6), :],
            q_ref[LANES * n : LANES * (n + 1), :],
            (((1,), (1,)), ((), ())),
            preferred_element_type=F32,
        )
        built = product[:48]
        for i in range(1, 6):
            begin = 24 * (start + i) - LANES * n
            built = jnp.where(lane >= begin, product[48 * i : 48 * (i + 1)], built)
        lanes = slice(LANES * n, LANES * (n + 1))
        out_ref[reader >> 1, reader & 1, :, lanes] = built.astype(BF16)

    thirds = (range(0, 5), range(5, 10), range(10, 16))
    ready = prepare(0, buffers[0])
    for third in thirds:
        ready(third)

    @pl.loop(0, 16, unroll=8)
    def _(pair):
        for side in range(2):
            reader = 2 * pair + side
            following = prepare((reader + 1) & 31, buffers[1 - side])
            for n, third in enumerate(thirds):
                multiply(reader, buffers[side], n)
                following(third)


def vmem():
    return pl.BlockSpec(memory_space=pltpu.VMEM)


def smem():
    return pl.BlockSpec(memory_space=pltpu.SMEM)


def step(array, axes, by):
    size = lax.axis_size(axes)
    return lax.ppermute(array, axes, [(i, (i + by) % size) for i in range(size)])


def swap(array):
    return step(array, "core", 1)


def ring(array, crossed=False):
    pairs = []
    for z in range(8):
        up, down = (2 * z + 2) % 16, (2 * z - 2) % 16 + 1
        pairs += [(2 * z, down), (2 * z + 1, up)] if crossed else [(2 * z, up), (2 * z + 1, down)]
    return lax.ppermute(array, ("z", "core"), pairs)


def params(mib):
    return pltpu.CompilerParams(vmem_limit_bytes=mib * MIB)


BINS = jax.ShapeDtypeStruct((512, 24, 256), BF16)


def unpack(own, sib, bins, turn):
    operands = [own, sib] + ([] if bins is None else [bins])
    return pl.pallas_call(
        unpack_kernel,
        out_shape=BINS,
        grid=(1,),
        in_specs=[pl.BlockSpec((8, 144, LANES), lambda i: (0, 0, 0))] * 2
        + [pl.BlockSpec(memory_space=pl.ANY)] * (len(operands) - 2),
        out_specs=pl.BlockSpec((64, 24, 256), lambda i: (turn, 0, 0)),
        input_output_aliases={} if bins is None else {2: 0},
        compiler_params=params(8),
        cost_estimate=pl.CostEstimate(flops=1500000000, bytes_accessed=2000000, transcendentals=0),
        name="unpack",
    )(*operands)


def grams(slots, own_tile, sib_tile, bins):
    return pl.pallas_call(
        grams_kernel,
        out_shape=jax.ShapeDtypeStruct((16, 2, 48, 384), BF16),
        in_specs=[smem()] + [vmem()] * 3,
        out_specs=vmem(),
        scratch_shapes=[pltpu.VMEM((768, 256), BF16), pltpu.VMEM((384, 256), BF16)] * 2,
        compiler_params=params(12),
        cost_estimate=pl.CostEstimate(
            flops=12000000000, bytes_accessed=8000000, transcendentals=0
        ),
        name="grams",
    )(slots, own_tile, sib_tile, bins)


def body(modes, point_weights, triads, counts):
    pieces = pl.pallas_call(
        split_kernel,
        out_shape=jax.ShapeDtypeStruct((8, 152, LANES), BF16),
        in_specs=[vmem()] * 3,
        out_specs=vmem(),
        compiler_params=params(56),
        name="split",
    )(modes.reshape(48, 24, LANES), triads[:, 0], point_weights[None])
    received = lax.all_to_all(pieces, ("x", "yh"), 0, 0)
    codes = received[:, 144:, :32].astype(F32)
    seconds = (codes[:, :, :16] * 64 + codes[:, :, 16:]).astype(jnp.int32)
    depth, core = lax.axis_index("z"), lax.axis_index("core")
    shape = (8, 8, 1)
    firsts = lax.broadcasted_iota(jnp.int32, shape, 1) * 64
    firsts = firsts + lax.broadcasted_iota(jnp.int32, shape, 0) * 8 + depth
    both = jnp.concatenate([seconds, (firsts + seconds) & 511], axis=2)
    turn = ((1 - 2 * core) * (depth - (both & 7))) & 7
    slots = (turn * 64 + (both & 56) + (both >> 6)).reshape(64, 32)

    beside = swap(received)
    near, sib = [received[:, :144]], [beside[:, :144]]
    near.append(ring(near[0]))
    sib.append(ring(near[0], crossed=True))
    for _ in range(2):
        near.append(ring(near[-1]))
        sib.append(ring(sib[-1]))
    near.append(ring(near[-1]))
    bins = unpack(near[0], sib[0], None, 0)
    passed = []
    for s in range(1, 4):
        pair = lax.optimization_barrier((sib[s], near[s]))
        passed.append((swap(pair[0]), swap(pair[1])))
    bins = unpack(near[1], sib[1], bins, 1)
    bins = unpack(*passed[0], bins, 7)
    bins = unpack(near[2], sib[2], bins, 2)
    bins = unpack(*passed[1], bins, 6)
    bins = unpack(near[3], sib[3], bins, 3)
    last, bins = lax.optimization_barrier((near[4], bins))
    last_passed = swap(last)
    bins = unpack(*passed[2], bins, 5)
    bins = unpack(last, last_passed, bins, 4)

    partial = grams(slots, received[0, 144:], beside[0, 144:], bins)
    parts = lax.all_to_all(partial, ("x", "yh", "yl"), 0, 0)
    parts, counts = lax.optimization_barrier((parts, counts))
    summed = jnp.sum(parts.astype(F32), axis=0) / 24
    rows = summed.reshape(2, 48, 16, 24).transpose(0, 2, 1, 3).reshape(2, 1, 16, 1152)
    gathered = lax.all_gather(rows, ("yl", "core"), tiled=True)
    live = jnp.arange(16, dtype=jnp.int32)[None, None, :, None] < counts[:, :, None, None]
    return jnp.where(live, gathered, 0.0)


def solution(mesh):
    fine = Mesh(mesh.devices.reshape(4, 2, 8, 2, 2), ("x", "yh", "z", "yl", "core"))
    freq, space = ("x", "yh", "z"), ("yl", "core")
    return jax.shard_map(
        body,
        mesh=fine,
        in_specs=(
            P(None, freq, None, None, None, space),
            P(space),
            P(None, freq, None),
            P(None, freq),
        ),
        out_specs=P(None, freq, None, None),
        check_vma=False,
    )
```

```python
import jax
import jax.numpy as jnp
from jax import lax
from jax.experimental import pallas as pl
from jax.experimental.pallas import tpu as pltpu
from jax.sharding import Mesh
from jax.sharding import PartitionSpec as P

F32, BF16 = jnp.float32, jnp.bfloat16
LANES = 128
MIB = 1024 * 1024


def split_kernel(x_ref, triads_ref, weights_ref, out_ref):
    block = lax.broadcasted_iota(jnp.int32, (24, LANES), 1) // 16
    for q in range(6):
        sources = [x_ref[8 * q + s].astype(F32) for s in range(8)]
        for bit in (1, 2, 4):
            high = (block & bit) > 0
            for s in range(8):
                if not s & bit:
                    low_part, high_part = sources[s], sources[s | bit]
                    raised = pltpu.roll(high_part, 16 * bit, 1)
                    lowered = pltpu.roll(low_part, LANES - 16 * bit, 1)
                    sources[s] = jnp.where(high, raised, low_part)
                    sources[s | bit] = jnp.where(high, high_part, lowered)
        for piece in range(8):
            out_ref[piece, 24 * q : 24 * q + 24] = sources[piece].astype(BF16)
    listed = triads_ref[...]
    rest = weights_ref[...]
    parts = []
    for _ in range(3):
        parts.append(rest.astype(BF16))
        rest = rest - parts[-1].astype(F32)
    for piece in range(8):
        tile = [(listed >> 6).astype(F32), (listed & 63).astype(F32)]
        for part in parts:
            own = part[:, 16 * piece : 16 * piece + 16].astype(F32)
            tile.append(jnp.broadcast_to(own, (8, 16)))
        tile.append(jnp.zeros((8, 48), F32))
        out_ref[piece, 144:152] = jnp.concatenate(tile, axis=1).astype(BF16)


def unpack_kernel(own_ref, sib_ref, *refs):
    bins_ref = refs[-1]
    lane = lax.broadcasted_iota(jnp.int32, (24, LANES), 1)

    @pl.loop(0, 8, unroll=4)
    def _(column):
        tiles = [
            [ref[column, 24 * q : 24 * q + 24].astype(F32) for q in range(6)]
            for ref in (own_ref, sib_ref)
        ]
        for r in range(8):
            for part in range(2):
                q, offset = divmod(96 * r + 48 * part, LANES)
                halves = []
                for core in range(2):
                    picked = tiles[core][q]
                    if offset + 48 > LANES:
                        picked = jnp.where(lane >= offset, picked, tiles[core][q + 1])
                    shift = (48 * core - offset) % LANES
                    halves.append(pltpu.roll(picked, shift, 1) if shift else picked)
                merged = jnp.where(lane < 48, halves[0], halves[1])
                lanes = slice(LANES * part, LANES * (part + 1))
                bins_ref[column * 8 + r, :, lanes] = merged.astype(BF16)


def lane_weights(own_ref, sib_ref):
    lane = lax.broadcasted_iota(jnp.int32, (8, LANES), 1)
    total = jnp.zeros((8, LANES), F32)
    for core, ref in enumerate((own_ref, sib_ref)):
        tile = ref[...].astype(F32)
        for component in range(3):
            begin = 48 * core + 16 * component
            inside = (lane >= begin) & (lane < begin + 16)
            value = sum(pltpu.roll(tile, (begin - 32 - 16 * n) % LANES, 1) for n in range(3))
            total = jnp.where(inside, value, total)
    return total[0:1]


def grams_kernel(slots_ref, own_w_ref, sib_w_ref, bins_ref, out_ref, *scratch):
    buffers = (scratch[0:2], scratch[2:4])
    core = lax.axis_index("core")
    weights = lane_weights(own_w_ref, sib_w_ref)
    lane = lax.broadcasted_iota(jnp.int32, (48, LANES), 1)

    def prepare(reader, buffer):
        w_ref, q_ref = buffer
        owner = reader >> 2
        row = (reader & 2) * 2 + core * 2 + (reader & 1)
        listed = owner * 8 + row
        first = bins_ref[listed].astype(F32)
        k_real = first[:, :LANES] * weights
        k_imag = first[:, LANES:] * weights

        def some(triads):
            for t in triads:
                second = bins_ref[slots_ref[listed, t]].astype(F32)
                l_real, l_imag = second[:, :LANES], second[:, LANES:]
                real = (k_real * l_real - k_imag * l_imag).astype(BF16)
                imag = k_real * l_imag + k_imag * l_real
                plus, minus = imag.astype(BF16), (-imag).astype(BF16)
                w_ref[48 * t : 48 * t + 24, :LANES] = real
                w_ref[48 * t : 48 * t + 24, LANES:] = plus
                w_ref[48 * t + 24 : 48 * t + 48, :LANES] = minus
                w_ref[48 * t + 24 : 48 * t + 48, LANES:] = real
                q_ref[24 * t : 24 * t + 24, :] = bins_ref[slots_ref[listed, 16 + t]]

        return some

    def multiply(reader, buffer, n):
        w_ref, q_ref = buffer
        start = 5 * n
        product = lax.dot_general(
            w_ref[48 * start : 48 * (start + 6), :],
            q_ref[LANES * n : LANES * (n + 1), :],
            (((1,), (1,)), ((), ())),
            preferred_element_type=F32,
        )
        built = product[:48]
        for i in range(1, 6):
            begin = 24 * (start + i) - LANES * n
            built = jnp.where(lane >= begin, product[48 * i : 48 * (i + 1)], built)
        lanes = slice(LANES * n, LANES * (n + 1))
        out_ref[reader >> 1, reader & 1, :, lanes] = built.astype(BF16)

    thirds = (range(0, 5), range(5, 10), range(10, 16))
    ready = prepare(0, buffers[0])
    for third in thirds:
        ready(third)

    @pl.loop(0, 16, unroll=8)
    def _(pair):
        for side in range(2):
            reader = 2 * pair + side
            following = prepare((reader + 1) & 31, buffers[1 - side])
            for n, third in enumerate(thirds):
                multiply(reader, buffers[side], n)
                following(third)


def vmem():
    return pl.BlockSpec(memory_space=pltpu.VMEM)


def smem():
    return pl.BlockSpec(memory_space=pltpu.SMEM)


def step(array, axes, by):
    size = lax.axis_size(axes)
    return lax.ppermute(array, axes, [(i, (i + by) % size) for i in range(size)])


def swap(array):
    return step(array, "core", 1)


def ring(array, crossed=False):
    pairs = []
    for z in range(8):
        up, down = (2 * z + 2) % 16, (2 * z - 2) % 16 + 1
        pairs += [(2 * z, down), (2 * z + 1, up)] if crossed else [(2 * z, up), (2 * z + 1, down)]
    return lax.ppermute(array, ("z", "core"), pairs)


def params(mib):
    return pltpu.CompilerParams(vmem_limit_bytes=mib * MIB)


BINS = jax.ShapeDtypeStruct((512, 24, 256), BF16)


def unpack(own, sib, bins, turn):
    operands = [own, sib] + ([] if bins is None else [bins])
    return pl.pallas_call(
        unpack_kernel,
        out_shape=BINS,
        grid=(1,),
        in_specs=[pl.BlockSpec((8, 144, LANES), lambda i: (0, 0, 0))] * 2
        + [pl.BlockSpec(memory_space=pl.ANY)] * (len(operands) - 2),
        out_specs=pl.BlockSpec((64, 24, 256), lambda i: (turn, 0, 0)),
        input_output_aliases={} if bins is None else {2: 0},
        compiler_params=params(8),
        cost_estimate=pl.CostEstimate(flops=1500000000, bytes_accessed=2000000, transcendentals=0),
        name="unpack",
    )(*operands)


def grams(slots, own_tile, sib_tile, bins):
    return pl.pallas_call(
        grams_kernel,
        out_shape=jax.ShapeDtypeStruct((16, 2, 48, 384), BF16),
        in_specs=[smem()] + [vmem()] * 3,
        out_specs=vmem(),
        scratch_shapes=[pltpu.VMEM((768, 256), BF16), pltpu.VMEM((384, 256), BF16)] * 2,
        compiler_params=params(12),
        cost_estimate=pl.CostEstimate(
            flops=12000000000, bytes_accessed=8000000, transcendentals=0
        ),
        name="grams",
    )(slots, own_tile, sib_tile, bins)


def body(modes, point_weights, triads, counts):
    pieces = pl.pallas_call(
        split_kernel,
        out_shape=jax.ShapeDtypeStruct((8, 152, LANES), BF16),
        in_specs=[vmem()] * 3,
        out_specs=vmem(),
        compiler_params=params(8),
        name="split",
    )(modes.reshape(48, 24, LANES), triads[:, 0], point_weights[None])
    received = lax.all_to_all(pieces, ("x", "yh"), 0, 0)
    codes = received[:, 144:, :32].astype(F32)
    seconds = (codes[:, :, :16] * 64 + codes[:, :, 16:]).astype(jnp.int32)
    depth, core = lax.axis_index("z"), lax.axis_index("core")
    shape = (8, 8, 1)
    firsts = lax.broadcasted_iota(jnp.int32, shape, 1) * 64
    firsts = firsts + lax.broadcasted_iota(jnp.int32, shape, 0) * 8 + depth
    both = jnp.concatenate([seconds, (firsts + seconds) & 511], axis=2)
    turn = ((1 - 2 * core) * (depth - (both & 7))) & 7
    slots = (turn * 64 + (both & 56) + (both >> 6)).reshape(64, 32)

    beside = swap(received)
    near, sib = [received[:, :144]], [beside[:, :144]]
    near.append(ring(near[0]))
    sib.append(ring(near[0], crossed=True))
    for _ in range(2):
        near.append(ring(near[-1]))
        sib.append(ring(sib[-1]))
    near.append(ring(near[-1]))
    bins = unpack(near[0], sib[0], None, 0)
    passed = []
    for s in range(1, 4):
        pair = lax.optimization_barrier((sib[s], near[s]))
        passed.append((swap(pair[0]), swap(pair[1])))
    bins = unpack(near[1], sib[1], bins, 1)
    bins = unpack(*passed[0], bins, 7)
    bins = unpack(near[2], sib[2], bins, 2)
    bins = unpack(*passed[1], bins, 6)
    bins = unpack(near[3], sib[3], bins, 3)
    last, bins = lax.optimization_barrier((near[4], bins))
    last_passed = swap(last)
    bins = unpack(*passed[2], bins, 5)
    bins = unpack(last, last_passed, bins, 4)

    partial = grams(slots, received[0, 144:], beside[0, 144:], bins)
    parts = lax.all_to_all(partial, ("x", "yh", "yl"), 0, 0)
    parts, counts = lax.optimization_barrier((parts, counts))
    summed = jnp.sum(parts.astype(F32), axis=0) / 24
    rows = summed.reshape(2, 48, 16, 24).transpose(0, 2, 1, 3).reshape(2, 1, 16, 1152)
    gathered = lax.all_gather(rows, ("yl", "core"), tiled=True)
    live = jnp.arange(16, dtype=jnp.int32)[None, None, :, None] < counts[:, :, None, None]
    return jnp.where(live, gathered, 0.0)


def solution(mesh):
    fine = Mesh(mesh.devices.reshape(4, 2, 8, 2, 2), ("x", "yh", "z", "yl", "core"))
    freq, space = ("x", "yh", "z"), ("yl", "core")
    return jax.shard_map(
        body,
        mesh=fine,
        in_specs=(
            P(None, freq, None, None, None, space),
            P(space),
            P(None, freq, None),
            P(None, freq),
        ),
        out_specs=P(None, freq, None, None),
        check_vma=False,
    )
```

```python
import jax
import jax.numpy as jnp
from jax import lax
from jax.experimental import pallas as pl
from jax.experimental.pallas import tpu as pltpu
from jax.sharding import Mesh
from jax.sharding import PartitionSpec as P

F32, BF16 = jnp.float32, jnp.bfloat16
LANES = 128
MIB = 1024 * 1024


def split_kernel(x_ref, triads_ref, weights_ref, out_ref):
    block = lax.broadcasted_iota(jnp.int32, (24, LANES), 1) // 16
    for q in range(6):
        sources = [x_ref[8 * q + s].astype(F32) for s in range(8)]
        for bit in (1, 2, 4):
            high = (block & bit) > 0
            for s in range(8):
                if not s & bit:
                    low_part, high_part = sources[s], sources[s | bit]
                    raised = pltpu.roll(high_part, 16 * bit, 1)
                    lowered = pltpu.roll(low_part, LANES - 16 * bit, 1)
                    sources[s] = jnp.where(high, raised, low_part)
                    sources[s | bit] = jnp.where(high, high_part, lowered)
        for piece in range(8):
            out_ref[piece, 24 * q : 24 * q + 24] = sources[piece].astype(BF16)
    listed = triads_ref[...]
    rest = weights_ref[...]
    parts = []
    for _ in range(3):
        parts.append(rest.astype(BF16))
        rest = rest - parts[-1].astype(F32)
    for piece in range(8):
        tile = [(listed >> 6).astype(F32), (listed & 63).astype(F32)]
        for part in parts:
            own = part[:, 16 * piece : 16 * piece + 16].astype(F32)
            tile.append(jnp.broadcast_to(own, (8, 16)))
        tile.append(jnp.zeros((8, 48), F32))
        out_ref[piece, 144:152] = jnp.concatenate(tile, axis=1).astype(BF16)


def unpack_kernel(own_ref, sib_ref, *refs):
    bins_ref = refs[-1]
    lane = lax.broadcasted_iota(jnp.int32, (24, LANES), 1)

    @pl.loop(0, 8, unroll=4)
    def _(column):
        tiles = [
            [ref[column, 24 * q : 24 * q + 24].astype(F32) for q in range(6)]
            for ref in (own_ref, sib_ref)
        ]
        for r in range(8):
            for part in range(2):
                q, offset = divmod(96 * r + 48 * part, LANES)
                halves = []
                for core in range(2):
                    picked = tiles[core][q]
                    if offset + 48 > LANES:
                        picked = jnp.where(lane >= offset, picked, tiles[core][q + 1])
                    shift = (48 * core - offset) % LANES
                    halves.append(pltpu.roll(picked, shift, 1) if shift else picked)
                merged = jnp.where(lane < 48, halves[0], halves[1])
                lanes = slice(LANES * part, LANES * (part + 1))
                bins_ref[column * 8 + r, :, lanes] = merged.astype(BF16)


def lane_weights(own_ref, sib_ref):
    lane = lax.broadcasted_iota(jnp.int32, (8, LANES), 1)
    total = jnp.zeros((8, LANES), F32)
    for core, ref in enumerate((own_ref, sib_ref)):
        tile = ref[...].astype(F32)
        for component in range(3):
            begin = 48 * core + 16 * component
            inside = (lane >= begin) & (lane < begin + 16)
            value = sum(pltpu.roll(tile, (begin - 32 - 16 * n) % LANES, 1) for n in range(3))
            total = jnp.where(inside, value, total)
    return total[0:1]


def grams_kernel(slots_ref, own_w_ref, sib_w_ref, bins_ref, out_ref, *scratch):
    buffers = (scratch[0:2], scratch[2:4])
    core = lax.axis_index("core")
    weights = lane_weights(own_w_ref, sib_w_ref)
    lane = lax.broadcasted_iota(jnp.int32, (48, LANES), 1)

    def prepare(reader, buffer):
        w_ref, q_ref = buffer
        owner = reader >> 2
        row = (reader & 2) * 2 + core * 2 + (reader & 1)
        listed = owner * 8 + row
        first = bins_ref[listed].astype(F32)
        k_real = first[:, :LANES] * weights
        k_imag = first[:, LANES:] * weights

        def some(triads):
            for t in triads:
                second = bins_ref[slots_ref[listed, t]].astype(F32)
                l_real, l_imag = second[:, :LANES], second[:, LANES:]
                real = (k_real * l_real - k_imag * l_imag).astype(BF16)
                imag = k_real * l_imag + k_imag * l_real
                plus = imag.astype(BF16)
                minus = -plus
                w_ref[48 * t : 48 * t + 24, :LANES] = real
                w_ref[48 * t : 48 * t + 24, LANES:] = plus
                w_ref[48 * t + 24 : 48 * t + 48, :LANES] = minus
                w_ref[48 * t + 24 : 48 * t + 48, LANES:] = real
                q_ref[24 * t : 24 * t + 24, :] = bins_ref[slots_ref[listed, 16 + t]]

        return some

    def multiply(reader, buffer, n):
        w_ref, q_ref = buffer
        start = 5 * n
        product = lax.dot_general(
            w_ref[48 * start : 48 * (start + 6), :],
            q_ref[LANES * n : LANES * (n + 1), :],
            (((1,), (1,)), ((), ())),
            preferred_element_type=F32,
        )
        built = product[:48]
        for i in range(1, 6):
            begin = 24 * (start + i) - LANES * n
            built = jnp.where(lane >= begin, product[48 * i : 48 * (i + 1)], built)
        lanes = slice(LANES * n, LANES * (n + 1))
        out_ref[reader >> 1, reader & 1, :, lanes] = built.astype(BF16)

    thirds = (range(0, 5), range(5, 10), range(10, 16))
    ready = prepare(0, buffers[0])
    for third in thirds:
        ready(third)

    @pl.loop(0, 16, unroll=8)
    def _(pair):
        for side in range(2):
            reader = 2 * pair + side
            following = prepare((reader + 1) & 31, buffers[1 - side])
            for n, third in enumerate(thirds):
                multiply(reader, buffers[side], n)
                following(third)


def vmem():
    return pl.BlockSpec(memory_space=pltpu.VMEM)


def smem():
    return pl.BlockSpec(memory_space=pltpu.SMEM)


def step(array, axes, by):
    size = lax.axis_size(axes)
    return lax.ppermute(array, axes, [(i, (i + by) % size) for i in range(size)])


def swap(array):
    return step(array, "core", 1)


def ring(array, crossed=False):
    pairs = []
    for z in range(8):
        up, down = (2 * z + 2) % 16, (2 * z - 2) % 16 + 1
        pairs += [(2 * z, down), (2 * z + 1, up)] if crossed else [(2 * z, up), (2 * z + 1, down)]
    return lax.ppermute(array, ("z", "core"), pairs)


def params(mib):
    return pltpu.CompilerParams(vmem_limit_bytes=mib * MIB)


BINS = jax.ShapeDtypeStruct((512, 24, 256), BF16)


def unpack(own, sib, bins, turn):
    operands = [own, sib] + ([] if bins is None else [bins])
    return pl.pallas_call(
        unpack_kernel,
        out_shape=BINS,
        grid=(1,),
        in_specs=[pl.BlockSpec((8, 144, LANES), lambda i: (0, 0, 0))] * 2
        + [pl.BlockSpec(memory_space=pl.ANY)] * (len(operands) - 2),
        out_specs=pl.BlockSpec((64, 24, 256), lambda i: (turn, 0, 0)),
        input_output_aliases={} if bins is None else {2: 0},
        compiler_params=params(8),
        cost_estimate=pl.CostEstimate(flops=1500000000, bytes_accessed=2000000, transcendentals=0),
        name="unpack",
    )(*operands)


def grams(slots, own_tile, sib_tile, bins):
    return pl.pallas_call(
        grams_kernel,
        out_shape=jax.ShapeDtypeStruct((16, 2, 48, 384), BF16),
        in_specs=[smem()] + [vmem()] * 3,
        out_specs=vmem(),
        scratch_shapes=[pltpu.VMEM((768, 256), BF16), pltpu.VMEM((384, 256), BF16)] * 2,
        compiler_params=params(12),
        cost_estimate=pl.CostEstimate(
            flops=12000000000, bytes_accessed=8000000, transcendentals=0
        ),
        name="grams",
    )(slots, own_tile, sib_tile, bins)


def body(modes, point_weights, triads, counts):
    pieces = pl.pallas_call(
        split_kernel,
        out_shape=jax.ShapeDtypeStruct((8, 152, LANES), BF16),
        in_specs=[vmem()] * 3,
        out_specs=vmem(),
        compiler_params=params(56),
        name="split",
    )(modes.reshape(48, 24, LANES), triads[:, 0], point_weights[None])
    received = lax.all_to_all(pieces, ("x", "yh"), 0, 0)
    codes = received[:, 144:, :32].astype(F32)
    seconds = (codes[:, :, :16] * 64 + codes[:, :, 16:]).astype(jnp.int32)
    depth, core = lax.axis_index("z"), lax.axis_index("core")
    shape = (8, 8, 1)
    firsts = lax.broadcasted_iota(jnp.int32, shape, 1) * 64
    firsts = firsts + lax.broadcasted_iota(jnp.int32, shape, 0) * 8 + depth
    both = jnp.concatenate([seconds, (firsts + seconds) & 511], axis=2)
    turn = ((1 - 2 * core) * (depth - (both & 7))) & 7
    slots = (turn * 64 + (both & 56) + (both >> 6)).reshape(64, 32)

    beside = swap(received)
    near, sib = [received[:, :144]], [beside[:, :144]]
    near.append(ring(near[0]))
    sib.append(ring(near[0], crossed=True))
    for _ in range(2):
        near.append(ring(near[-1]))
        sib.append(ring(sib[-1]))
    near.append(ring(near[-1]))
    bins = unpack(near[0], sib[0], None, 0)
    passed = []
    for s in range(1, 4):
        pair = lax.optimization_barrier((sib[s], near[s]))
        passed.append((swap(pair[0]), swap(pair[1])))
    bins = unpack(near[1], sib[1], bins, 1)
    bins = unpack(*passed[0], bins, 7)
    bins = unpack(near[2], sib[2], bins, 2)
    bins = unpack(*passed[1], bins, 6)
    bins = unpack(near[3], sib[3], bins, 3)
    last, bins = lax.optimization_barrier((near[4], bins))
    last_passed = swap(last)
    bins = unpack(*passed[2], bins, 5)
    bins = unpack(last, last_passed, bins, 4)

    partial = grams(slots, received[0, 144:], beside[0, 144:], bins)
    parts = lax.all_to_all(partial, ("x", "yh", "yl"), 0, 0)
    parts, counts = lax.optimization_barrier((parts, counts))
    summed = jnp.sum(parts.astype(F32), axis=0) / 24
    rows = summed.reshape(2, 48, 16, 24).transpose(0, 2, 1, 3).reshape(2, 1, 16, 1152)
    gathered = lax.all_gather(rows, ("yl", "core"), tiled=True)
    live = jnp.arange(16, dtype=jnp.int32)[None, None, :, None] < counts[:, :, None, None]
    return jnp.where(live, gathered, 0.0)


def solution(mesh):
    fine = Mesh(mesh.devices.reshape(4, 2, 8, 2, 2), ("x", "yh", "z", "yl", "core"))
    freq, space = ("x", "yh", "z"), ("yl", "core")
    return jax.shard_map(
        body,
        mesh=fine,
        in_specs=(
            P(None, freq, None, None, None, space),
            P(space),
            P(None, freq, None),
            P(None, freq),
        ),
        out_specs=P(None, freq, None, None),
        check_vma=False,
    )
```
